256 devices in a mesh: seq: 64 (over z, x, core), grp: 4 (over y).
Axes of the slice: x: 4, y: 4, z: 8, core: 2. Of those that a mesh axis runs over, the one named last changes fastest.
Arguments:
- streams: float32 [3, 16384, 4096], P(None, 'seq', 'grp'), may hold values from -6 to 6
- short_filters: float32 [3, 3, 4096], P(None, None, 'grp'), may hold values from -3.5 to 3.5
- skip_gain: float32 [4096], P('grp'), may hold values from -4 to 4
- long_filter: float32 [16384, 256], P('seq', 'grp'), may hold values from -0.046875 to 0.046875
Outputs:
- hyena_output: float32 [256, 64, 4096], P('seq', None, 'grp')
The draws below stay inside these ranges and needn't reach their ends.
All inputs are finite; a program needn't handle non-finite values.
Results may differ from the reference program's by a relative error of at most 0.00011.
Values sent between devices are 32-bit elements; how exact they have to be, the bound alone decides.
A program may use at most 64 MiB of HBM per device.

```python
import jax
import jax.numpy as jnp
from jax import lax

D = 4096
FILTERS = 256
TOK_DEV = 256
PANELS = 64
TOKENS = 16384


def levels(own_key, dims, pieces, least, largest):
    factor_of = 1.0
    for position, parts in pieces:
        heights = jax.random.uniform(jax.random.fold_in(jax.random.fold_in(own_key, 6), position), (parts,), jnp.float32, least / len(pieces), largest / len(pieces))
        factor_of = factor_of * jnp.repeat(jnp.exp(heights), dims[position] // parts).reshape((-1,) + (1,) * (len(dims) - 1 - position))
    return factor_of


def scatter_about(stream_key, dims, width, most, pieces=(), dtype=jnp.bfloat16):
    array = jax.random.normal(stream_key, dims, jnp.float32) * width
    if len(pieces) > 0:
        array = levels(stream_key, dims, pieces, -0.22, 0.18) * array
    return jnp.clip(array, min=-most, max=most).astype(dtype)


def setup_inputs(seed: int = 0) -> dict:
    arg_keys = jax.random.split(jax.random.key(seed), 5)
    streams = scatter_about(arg_keys[0], (3, TOKENS, D), 1.0, 6.0, ((1, 64), (2, 4)), jnp.float32)
    short_filters = scatter_about(arg_keys[1], (3, 3, D), 3 ** -0.5, 3.5, ((2, 4),), jnp.float32)
    skip_gain = scatter_about(arg_keys[2], (D,), 1.0, 4.0, ((0, 4),), jnp.float32)
    long_filter = scatter_about(arg_keys[3], (TOKENS, FILTERS), TOKENS ** -0.5, 0.046875, ((0, 64), (1, 4)), jnp.float32)
    return {"streams": streams, "short_filters": short_filters, "skip_gain": skip_gain, "long_filter": long_filter}


def featurize(streams, short_filters):
    length = streams.shape[1]
    padded = jnp.pad(streams, ((0, 0), (2, 0), (0, 0)))
    return (short_filters[:, 0:1, :] * padded[:, 2:, :]
            + short_filters[:, 1:2, :] * padded[:, 1:length + 1, :]
            + short_filters[:, 2:3, :] * padded[:, 0:length, :])


def reference(streams, short_filters, skip_gain, long_filter):
    featured = featurize(streams, short_filters)
    query_rows = featured[0]
    gated_rows = featured[1] * featured[2]
    points = 2 * TOKENS
    blocks = gated_rows.reshape(TOKENS, D // FILTERS, FILTERS).transpose(2, 0, 1)
    filter_cols = long_filter.T

    def convolve(operands):
        block_rows, filter_taps = operands
        spectrum = jnp.fft.rfft(block_rows, n=points, axis=0) * jnp.fft.rfft(filter_taps, n=points)[:, None]
        return jnp.fft.irfft(spectrum, n=points, axis=0)[:TOKENS]

    convolved = lax.map(convolve, (blocks, filter_cols))
    convolved = convolved.transpose(1, 2, 0).reshape(TOKENS, D)
    output_rows = query_rows * (convolved + skip_gain * gated_rows)
    return output_rows.reshape(PANELS, TOK_DEV, D).transpose(1, 0, 2)
```

```python
import functools

import jax
import jax.numpy as jnp
import ml_dtypes
import numpy as np
from jax import lax
from jax.experimental import pallas as pl
from jax.experimental.pallas import tpu as pltpu
from jax.sharding import PartitionSpec as P

MESH = pl.DeviceIdType.MESH
SEQ = 64
GRP = 4
TOK = 256
CH = 1024
POINTS = SEQ * TOK
QUARTERS = 4
LANES = 128


def split_parts(matrix):
    high = matrix.astype(ml_dtypes.bfloat16)
    low = (matrix - high.astype(np.float64)).astype(ml_dtypes.bfloat16)
    return high, low


@functools.cache
def tables():
    r = np.arange(SEQ)
    k1 = np.arange(SEQ)
    m = np.arange(TOK)
    k2 = np.arange(TOK)
    column = np.arange(TOK)
    m_of = 4 * (column % 64) + 2 * ((column // 64) % 2) + column // 128
    coarse = 2 * np.pi * np.outer(k1 + 0.25, r) / SEQ
    head = np.concatenate([np.cos(coarse), -np.sin(coarse)], axis=0)
    head_high, head_low = split_parts(head)
    head_all = np.concatenate([head_high, head_high, head_low], axis=1)
    tail = np.concatenate([np.cos(coarse.T), -np.sin(coarse.T)], axis=1)
    tail_high, tail_low = split_parts(tail)
    tail_all = np.concatenate([tail_high, tail_high, tail_low], axis=1)
    twist = 2 * np.pi * np.outer(k1 + 0.25, m) / POINTS
    turn = 2 * np.pi * np.outer(k1 + 0.25, m_of) / POINTS
    twists = np.stack(
        [np.cos(twist), -np.sin(twist), np.cos(turn) / POINTS, np.sin(turn) / POINTS]
    ).astype(np.float32)
    fine = 2 * np.pi * (np.outer(m, k2) % TOK) / TOK
    fine_cos, fine_sin = np.cos(fine), -np.sin(fine)
    forward = np.block([[fine_cos, fine_sin], [-fine_sin, fine_cos]])
    back = 2 * np.pi * (np.outer(k2, m_of) % TOK) / TOK
    back_cos, back_sin = np.cos(back), np.sin(back)
    inverse = np.block([[back_cos, back_sin], [-back_sin, back_cos]])
    wide = np.stack([*split_parts(forward), *split_parts(inverse)])
    return head_all, tail_all, twists, wide


def halves(values):
    high = values.astype(jnp.bfloat16)
    low = (values - high.astype(jnp.float32)).astype(jnp.bfloat16)
    return high, low


def product(left, right):
    return jnp.dot(left, right, preferred_element_type=jnp.float32)


def kernel(
    streams_hbm, taps_hbm, gain_hbm, filter_hbm, head_hbm, tail_hbm, twist_hbm, wide_hbm,
    out_ref,
    stream, taps, gain, filt, head, tail, twist, wide,
    rim_send, rim_recv, filt_send, filt_recv, filt_all, response,
    gate_send, gate_recv, query_send, query_recv, conv_send, conv_recv,
    load_sem, rim_sems, filt_sems, ring_sems, gate_out, gate_in, query_sems, conv_out, conv_in,
):
    me = lax.axis_index("seq")
    group = lax.axis_index("grp")
    barrier = pltpu.get_barrier_semaphore()

    def greet(step, carry):
        other = lax.rem(me + step, SEQ)
        pl.semaphore_signal(barrier, inc=1, device_id=(other, group), device_id_type=MESH)
        return carry

    def greet_group(step, carry):
        other = lax.rem(group + step, GRP)
        pl.semaphore_signal(barrier, inc=1, device_id=(me, other), device_id_type=MESH)
        return carry

    def load(source, target, slot):
        return pltpu.make_async_copy(source, target, load_sem.at[slot])

    def stream_load(block):
        lanes = pl.ds(block * LANES, LANES)
        return load(streams_hbm.at[:, :, lanes], stream.at[:, block, pl.ds(8, TOK), :], block)

    for block in range(8):
        stream_load(block).start()
    small_loads = [
        load(filter_hbm, filt, 8),
        load(taps_hbm, taps, 9),
        load(gain_hbm, gain, 10),
        load(head_hbm, head, 11),
        load(tail_hbm, tail, 12),
        load(twist_hbm, twist, 13),
        load(wide_hbm, wide, 14),
    ]
    for copy in small_loads:
        copy.start()
    lax.fori_loop(1, SEQ, greet, 0)
    lax.fori_loop(1, GRP, greet_group, 0)

    small_loads[0].wait()
    for half in range(2):
        turned = jnp.transpose(filt[pl.ds(half * LANES, LANES), :])
        filt_send[:, half, :] = turned
    for block in range(8):
        stream_load(block).wait()
    rim_send[...] = jnp.zeros_like(rim_send)
    for s in range(3):
        rim_send[:, pl.ds(2 * s, 2), :] = stream[s, :, pl.ds(TOK + 6, 2), :]
    pl.semaphore_wait(barrier, SEQ - 1 + GRP - 1)

    def rim_copy(other):
        return pltpu.make_async_remote_copy(
            src_ref=rim_send, dst_ref=rim_recv, send_sem=rim_sems.at[0], recv_sem=rim_sems.at[1],
            device_id=(other, group), device_id_type=MESH,
        )

    @pl.when(me < SEQ - 1)
    def _():
        rim_copy(me + 1).start()

    def send_filter(step, carry):
        other = lax.rem(me + step, SEQ)
        pltpu.make_async_remote_copy(
            src_ref=filt_send.at[other], dst_ref=filt_recv.at[me],
            send_sem=filt_sems.at[0], recv_sem=filt_sems.at[1],
            device_id=(other, group), device_id_type=MESH,
        ).start()
        return carry

    lax.fori_loop(1, SEQ, send_filter, 0)
    filt_recv[me] = filt_send[me]
    small_loads[1].wait()

    def feature(s, start, block, size, stride=None):
        lanes = pl.ds(pl.multiple_of(block * LANES, LANES), LANES)

        def rows(first):
            window = pl.ds(first, size) if stride is None else pl.ds(first, size, stride)
            return stream[s, block, window, :]

        return (
            taps[s, 0:1, lanes] * rows(start)
            + taps[s, 1:2, lanes] * rows(start - 1)
            + taps[s, 2:3, lanes] * rows(start - 2)
        )

    def gate(quarter, half):
        for pair in range(2):
            block = quarter * 2 + pair
            first = 8 + half * LANES
            gated = feature(1, first, block, LANES) * feature(2, first, block, LANES)
            turned = jnp.transpose(gated)
            for own in range(2):
                row = half * 4 + pair * 2 + own
                gate_send[quarter, pl.ds(row, SEQ, 8), :] = turned[own * 64 : own * 64 + 64]

    def gate_late(quarter, carry):
        gate(quarter, 1)
        return carry

    lax.fori_loop(0, QUARTERS, gate_late, 0)

    @pl.when(me > 0)
    def _():
        rim_copy(me).wait_recv()
        for s in range(3):
            stream[s, :, pl.ds(6, 2), :] = rim_recv[:, pl.ds(2 * s, 2), :]

    @pl.when(me == 0)
    def _():
        for s in range(3):
            stream[s, :, pl.ds(6, 2), :] = jnp.zeros((8, 2, LANES), jnp.float32)

    def gate_early(quarter, carry):
        gate(quarter, 0)

        def send(step, inner):
            other = lax.rem(me + step, SEQ)
            pltpu.make_async_remote_copy(
                src_ref=gate_send.at[quarter, pl.ds(pl.multiple_of(other * 8, 8), 8)],
                dst_ref=gate_recv.at[quarter, pl.ds(pl.multiple_of(me * 8, 8), 8)],
                send_sem=gate_out.at[quarter], recv_sem=gate_in.at[quarter],
                device_id=(other, group), device_id_type=MESH,
            ).start()
            return inner

        lax.fori_loop(1, SEQ, send, 0)
        own = pl.ds(pl.multiple_of(me * 8, 8), 8)
        gate_recv[quarter, own, :] = gate_send[quarter, own, :]
        return carry

    lax.fori_loop(0, QUARTERS, gate_early, 0)

    def query(block, carry):
        for low in range(4):
            featured = feature(0, 8 + low, block, SEQ, 4)
            query_send[pl.ds(low * 8 + block, SEQ, 32), :] = featured
        return carry

    lax.fori_loop(0, 8, query, 0)

    def send_query(step, carry):
        other = lax.rem(me + step, SEQ)
        pltpu.make_async_remote_copy(
            src_ref=query_send.at[pl.ds(pl.multiple_of(other * 32, 32), 32)],
            dst_ref=query_recv.at[pl.ds(pl.multiple_of(me * 32, 32), 32)],
            send_sem=query_sems.at[0], recv_sem=query_sems.at[1],
            device_id=(other, group), device_id_type=MESH,
        ).start()
        return carry

    lax.fori_loop(1, SEQ, send_query, 0)
    own_query = pl.ds(pl.multiple_of(me * 32, 32), 32)
    query_recv[own_query, :] = query_send[own_query, :]

    def wait_bytes(ref, sem):
        pltpu.make_async_copy(ref, ref, sem).wait()

    wait_bytes(filt_recv.at[pl.ds(0, SEQ - 1)], filt_sems.at[1])
    for half in range(2):
        filt_all[group, :, half * LANES : half * LANES + LANES] = filt_recv[:, half, :]

    def send_ring(step, carry):
        other = lax.rem(group + step, GRP)
        pltpu.make_async_remote_copy(
            src_ref=filt_all.at[group], dst_ref=filt_all.at[group],
            send_sem=ring_sems.at[0], recv_sem=ring_sems.at[1],
            device_id=(me, other), device_id_type=MESH,
        ).start()
        return carry

    lax.fori_loop(1, GRP, send_ring, 0)
    for copy in small_loads[2:]:
        copy.wait()

    def spectrum(rows_of):
        reals, imags = [], []
        for f in range(4):
            high, low = halves(rows_of(f))
            coarse = product(head[...], jnp.concatenate([high, low, high], axis=0))
            real, imag = coarse[:SEQ], coarse[SEQ:]
            reals.append(real * twist[0] - imag * twist[1])
            imags.append(real * twist[1] + imag * twist[0])
        both = jnp.concatenate(
            [jnp.concatenate(reals, axis=0), jnp.concatenate(imags, axis=0)], axis=1
        )
        high, low = halves(both)
        return product(high, wide[0]) + product(low, wide[0]) + product(high, wide[1])

    wait_bytes(filt_all.at[pl.ds(0, GRP - 1)], ring_sems.at[1])
    response[...] = spectrum(lambda f: filt_all[f])

    def convolve(quarter, carry):
        wait_bytes(gate_recv.at[quarter, pl.ds(0, (SEQ - 1) * 8)], gate_in.at[quarter])

        def rows_of(f):
            return jnp.concatenate(
                [gate_recv[quarter, pl.ds(f, SEQ, 8), :], gate_recv[quarter, pl.ds(4 + f, SEQ, 8), :]],
                axis=1,
            )

        signal = spectrum(rows_of)
        reals, imags = [], []
        for f in range(4):
            rows = slice(f * SEQ, f * SEQ + SEQ)
            real, imag = signal[rows, :TOK], signal[rows, TOK:]
            skip = gain[(quarter * 4 + f) * SEQ + me]
            tap_real = response[rows, :TOK] + skip
            tap_imag = response[rows, TOK:]
            reals.append(real * tap_real - imag * tap_imag)
            imags.append(real * tap_imag + imag * tap_real)
        both = jnp.concatenate(
            [jnp.concatenate(reals, axis=0), jnp.concatenate(imags, axis=0)], axis=1
        )
        high, low = halves(both)
        back = product(high, wide[2]) + product(low, wide[2]) + product(high, wide[3])
        for f in range(4):
            rows = slice(f * SEQ, f * SEQ + SEQ)
            real, imag = back[rows, :TOK], back[rows, TOK:]
            turned = jnp.concatenate(
                [real * twist[2] - imag * twist[3], real * twist[3] + imag * twist[2]], axis=0
            )
            high, low = halves(turned)
            result = product(tail[...], jnp.concatenate([high, low, high], axis=0))
            stacked = jnp.concatenate([result[:, :LANES], result[:, LANES:]], axis=0)
            flipped = jnp.transpose(stacked)
            for upper in range(2):
                conv_send[quarter, pl.ds(upper * 4 + f, SEQ, 8), :] = flipped[
                    upper * 64 : upper * 64 + 64
                ]

        def send(step, inner):
            other = lax.rem(me + step, SEQ)
            pltpu.make_async_remote_copy(
                src_ref=conv_send.at[quarter, pl.ds(pl.multiple_of(other * 8, 8), 8)],
                dst_ref=conv_recv.at[quarter, pl.ds(pl.multiple_of(me * 8, 8), 8)],
                send_sem=conv_out.at[quarter], recv_sem=conv_in.at[quarter],
                device_id=(other, group), device_id_type=MESH,
            ).start()
            return inner

        lax.fori_loop(1, SEQ, send, 0)
        own = pl.ds(pl.multiple_of(me * 8, 8), 8)
        conv_recv[quarter, own, :] = conv_send[quarter, own, :]
        return carry

    lax.fori_loop(0, QUARTERS, convolve, 0)

    wait_bytes(query_recv.at[pl.ds(0, (SEQ - 1) * 32)], query_sems.at[1])

    def finish(quarter, carry):
        wait_bytes(conv_recv.at[quarter, pl.ds(0, (SEQ - 1) * 8)], conv_in.at[quarter])
        for pair in range(2):
            block = quarter * 2 + pair
            lanes = pl.ds(pl.multiple_of(block * LANES, LANES), LANES)
            for upper in range(2):
                gathered = jnp.concatenate(
                    [conv_recv[quarter, pl.ds(upper * 4 + pair * 2 + own, SEQ, 8), :] for own in range(2)],
                    axis=0,
                )
                result = jnp.transpose(gathered)
                for lower in range(2):
                    offset = upper * 2 + lower
                    asked = query_recv[pl.ds(offset * 8 + block, SEQ, 32), :]
                    out_ref[offset, :, lanes] = asked * result[lower * 64 : lower * 64 + 64]
        return carry

    lax.fori_loop(0, QUARTERS, finish, 0)

    @pl.when(me < SEQ - 1)
    def _():
        rim_copy(me + 1).wait_send()

    wait_bytes(filt_send.at[pl.ds(0, SEQ - 1)], filt_sems.at[0])
    wait_bytes(filt_all.at[pl.ds(0, GRP - 1)], ring_sems.at[0])
    wait_bytes(query_send.at[pl.ds(0, (SEQ - 1) * 32)], query_sems.at[0])
    for quarter in range(QUARTERS):
        wait_bytes(gate_send.at[quarter, pl.ds(0, (SEQ - 1) * 8)], gate_out.at[quarter])
        wait_bytes(conv_send.at[quarter, pl.ds(0, (SEQ - 1) * 8)], conv_out.at[quarter])


def body(streams, short_filters, skip_gain, long_filter):
    head_all, tail_all, twists, wide = tables()
    dma = pltpu.SemaphoreType.DMA
    f32 = jnp.float32
    any_space = pl.BlockSpec(memory_space=pl.ANY)
    return pl.pallas_call(
        kernel,
        out_shape=jax.ShapeDtypeStruct((TOK // SEQ, SEQ, CH), f32),
        in_specs=[any_space] * 8,
        out_specs=pl.BlockSpec(memory_space=pltpu.VMEM),
        scratch_shapes=[
            pltpu.VMEM((3, 8, TOK + 8, LANES), f32),
            pltpu.VMEM((3, 3, CH), f32),
            pltpu.SMEM((CH,), f32),
            pltpu.VMEM((TOK, 64), f32),
            pltpu.VMEM(head_all.shape, jnp.bfloat16),
            pltpu.VMEM(tail_all.shape, jnp.bfloat16),
            pltpu.VMEM(twists.shape, f32),
            pltpu.VMEM(wide.shape, jnp.bfloat16),
            pltpu.VMEM((8, 8, LANES), f32),
            pltpu.VMEM((8, 8, LANES), f32),
            pltpu.VMEM((SEQ, 2, LANES), f32),
            pltpu.VMEM((SEQ, 2, LANES), f32),
            pltpu.VMEM((GRP, SEQ, TOK), f32),
            pltpu.VMEM((TOK, 2 * TOK), f32),
            pltpu.VMEM((QUARTERS, SEQ * 8, LANES), f32),
            pltpu.VMEM((QUARTERS, SEQ * 8, LANES), f32),
            pltpu.VMEM((SEQ * 32, LANES), f32),
            pltpu.VMEM((SEQ * 32, LANES), f32),
            pltpu.VMEM((QUARTERS, SEQ * 8, LANES), f32),
            pltpu.VMEM((QUARTERS, SEQ * 8, LANES), f32),
            dma((15,)),
            dma((2,)),
            dma((2,)),
            dma((2,)),
            dma((QUARTERS,)),
            dma((QUARTERS,)),
            dma((2,)),
            dma((QUARTERS,)),
            dma((QUARTERS,)),
        ],
        compiler_params=pltpu.CompilerParams(
            collective_id=0, has_side_effects=True, vmem_limit_bytes=48 << 20
        ),
    )(streams, short_filters, skip_gain, long_filter, head_all, tail_all, twists, wide)


def solution(mesh):
    return jax.shard_map(
        body,
        mesh=mesh,
        in_specs=(P(None, "seq", "grp"), P(None, None, "grp"), P("grp"), P("seq", "grp")),
        out_specs=P("seq", None, "grp"),
        check_vma=False,
    )
```

```python
import functools

import jax
import jax.numpy as jnp
import ml_dtypes
import numpy as np
from jax import lax
from jax.experimental import pallas as pl
from jax.experimental.pallas import tpu as pltpu
from jax.sharding import PartitionSpec as P

MESH = pl.DeviceIdType.MESH
SEQ = 64
GRP = 4
TOK = 256
CH = 1024
POINTS = SEQ * TOK
QUARTERS = 4
LANES = 128


def split_parts(matrix):
    high = matrix.astype(ml_dtypes.bfloat16)
    low = (matrix - high.astype(np.float64)).astype(ml_dtypes.bfloat16)
    return high, low


@functools.cache
def tables():
    r = np.arange(SEQ)
    k1 = np.arange(SEQ)
    m = np.arange(TOK)
    k2 = np.arange(TOK)
    column = np.arange(TOK)
    m_of = 4 * (column // 64 % 2 * 32 + column % 32) + 2 * (column // 32 % 2) + column // 128
    coarse = 2 * np.pi * np.outer(k1 + 0.25, r) / SEQ
    head = np.concatenate([np.cos(coarse), -np.sin(coarse)], axis=0)
    head_high, head_low = split_parts(head)
    head_all = np.concatenate([head_high, head_high, head_low], axis=1)
    tail = np.concatenate([np.cos(coarse.T), -np.sin(coarse.T)], axis=1)
    tail_high, tail_low = split_parts(tail)
    tail_all = np.concatenate([tail_high, tail_high, tail_low], axis=1)
    twist = 2 * np.pi * np.outer(k1 + 0.25, m) / POINTS
    turn = 2 * np.pi * np.outer(k1 + 0.25, m_of) / POINTS
    twists = np.stack(
        [np.cos(twist), -np.sin(twist), np.cos(turn) / POINTS, np.sin(turn) / POINTS]
    ).astype(np.float32)
    fine = 2 * np.pi * (np.outer(m, k2) % TOK) / TOK
    fine_cos, fine_sin = np.cos(fine), -np.sin(fine)
    forward = np.block([[fine_cos, fine_sin], [-fine_sin, fine_cos]])
    back = 2 * np.pi * (np.outer(k2, m_of) % TOK) / TOK
    back_cos, back_sin = np.cos(back), np.sin(back)
    inverse = np.block([[back_cos, back_sin], [-back_sin, back_cos]])
    wide = np.stack([*split_parts(forward), *split_parts(inverse)])
    return head_all, tail_all, twists, wide


def halves(values):
    high = values.astype(jnp.bfloat16)
    low = (values - high.astype(jnp.float32)).astype(jnp.bfloat16)
    return high, low


def product(left, right):
    return jnp.dot(left, right, preferred_element_type=jnp.float32)


def kernel(
    streams_hbm, taps_hbm, gain_hbm, filter_hbm, head_hbm, tail_hbm, twist_hbm, wide_hbm,
    out_hbm,
    stream, taps, gain, filt, head, tail, twist, wide,
    rim, filt_send, filt_recv, filt_all, response,
    gate_send, gate_recv, near_send, near_recv, far_send, far_recv, conv_send, conv_recv, result,
    load_sem, rim_sems, filt_sems, ring_sems, gate_out, gate_in, near_sems, far_sems,
    conv_out, conv_in, out_sem,
):
    me = lax.axis_index("seq")
    group = lax.axis_index("grp")
    plane, place, side = me // 8, lax.rem(me, 8), lax.rem(me, 2)
    far_plane = lax.rem(plane + 2 + side, 8)
    barrier = pltpu.get_barrier_semaphore()

    def load(source, target, slot):
        return pltpu.make_async_copy(source, target, load_sem.at[slot])

    def query_load(block):
        lanes = pl.ds(block * LANES, LANES)
        return load(streams_hbm.at[0, :, lanes], stream.at[0, block, pl.ds(8, TOK), :], block)

    def gate_load(block):
        lanes = pl.ds(block * LANES, LANES)
        return load(
            streams_hbm.at[pl.ds(1, 2), :, lanes],
            stream.at[pl.ds(1, 2), block, pl.ds(8, TOK), :],
            8 + block,
        )

    near_recv[...] = jnp.ones_like(near_recv)
    for s in range(3):
        stream[s, :, pl.ds(6, 2), :] = jnp.zeros((8, 2, LANES), jnp.float32)
    small_loads = [
        load(taps_hbm, taps, 16),
        load(filter_hbm, filt, 17),
        load(gain_hbm, gain, 18),
        load(head_hbm, head, 19),
        load(tail_hbm, tail, 20),
        load(twist_hbm, twist, 21),
        load(wide_hbm, wide, 22),
    ]
    small_loads[0].start()
    for block in range(8):
        query_load(block).start()
    small_loads[1].start()
    for block in range(8):
        gate_load(block).start()
    for copy in small_loads[2:]:
        copy.start()

    def greet(step, carry):
        other = lax.rem(me + step, SEQ)
        pl.semaphore_signal(barrier, inc=1, device_id=(other, group), device_id_type=MESH)
        return carry

    def greet_group(step, carry):
        other = lax.rem(group + step, GRP)
        pl.semaphore_signal(barrier, inc=1, device_id=(me, other), device_id_type=MESH)
        return carry

    lax.fori_loop(1, SEQ, greet, 0)
    lax.fori_loop(1, GRP, greet_group, 0)

    def wait_bytes(ref, sem):
        pltpu.make_async_copy(ref, ref, sem).wait()

    def feature(s, start, block, size, stride=None):
        lanes = pl.ds(pl.multiple_of(block * LANES, LANES), LANES)

        def rows(first):
            window = pl.ds(first, size) if stride is None else pl.ds(first, size, stride)
            return stream[s, block, window, :]

        return (
            taps[s, 0:1, lanes] * rows(start)
            + taps[s, 1:2, lanes] * rows(start - 1)
            + taps[s, 2:3, lanes] * rows(start - 2)
        )

    small_loads[0].wait()
    for block in range(8):
        query_load(block).wait()

    def near_query(block, carry):
        for step in range(4):
            goal = lax.rem(far_plane + 4 + step, 8)
            for low in range(4):
                featured = feature(0, 8 + goal * 32 + low, block, 8, 4)
                near_send[pl.ds(goal * 256 + low * 8 + block, 8, 32), :] = featured
        return carry

    lax.fori_loop(0, 8, near_query, 0)
    small_loads[1].wait()
    for half in range(2):
        filt_send[:, half, :] = filt[:, half * LANES : half * LANES + LANES]

    pl.semaphore_wait(barrier, SEQ - 1 + GRP - 1)

    def rim_copy(block, other):
        return pltpu.make_async_remote_copy(
            src_ref=streams_hbm.at[:, pl.ds(TOK - 8, 8), pl.ds(block * LANES, LANES)],
            dst_ref=rim.at[:, block], send_sem=rim_sems.at[0], recv_sem=rim_sems.at[1],
            device_id=(other, group), device_id_type=MESH,
        )

    @pl.when(me < SEQ - 1)
    def _():
        for block in range(8):
            rim_copy(block, me + 1).start()

    def near_copy(other):
        return pltpu.make_async_remote_copy(
            src_ref=near_send.at[pl.ds(pl.multiple_of(other * 32, 32), 32)],
            dst_ref=near_recv.at[pl.ds(pl.multiple_of(me * 32, 32), 32)],
            send_sem=near_sems.at[0], recv_sem=near_sems.at[1],
            device_id=(other, group), device_id_type=MESH,
        )

    def send_near(step, carry):
        goal = lax.rem(far_plane + 4 + lax.rem(step, 4), 8)
        other = goal * 8 + lax.rem(place + step // 4, 8)

        @pl.when((other != me) & (other != 0))
        def _():
            near_copy(other).start()

        return carry

    lax.fori_loop(0, 32, send_near, 0)

    def send_filter(step, carry):
        other = lax.rem(me + step, SEQ)
        pltpu.make_async_remote_copy(
            src_ref=filt_send.at[other], dst_ref=filt_recv.at[me],
            send_sem=filt_sems.at[0], recv_sem=filt_sems.at[1],
            device_id=(other, group), device_id_type=MESH,
        ).start()
        return carry

    lax.fori_loop(1, SEQ, send_filter, 0)
    filt_recv[me] = filt_send[me]
    for block in range(8):
        gate_load(block).wait()

    def gate(quarter, half):
        for pair in range(2):
            block = quarter * 2 + pair
            first = 8 + half * LANES
            gated = feature(1, first, block, LANES) * feature(2, first, block, LANES)
            turned = jnp.transpose(gated)
            for own in range(2):
                row = half * 4 + pair * 2 + own
                gate_send[quarter, pl.ds(row, SEQ, 8), :] = turned[own * 64 : own * 64 + 64]

    def gate_late(quarter, carry):
        gate(quarter, 1)
        return carry

    lax.fori_loop(0, QUARTERS, gate_late, 0)

    @pl.when(me > 0)
    def _():
        wait_bytes(rim, rim_sems.at[1])
        for s in range(3):
            stream[s, :, pl.ds(6, 2), :] = rim[s, :, pl.ds(6, 2), :]

    def gate_early(quarter, carry):
        gate(quarter, 0)

        def send(step, inner):
            other = lax.rem(me + step, SEQ)
            pltpu.make_async_remote_copy(
                src_ref=gate_send.at[quarter, pl.ds(pl.multiple_of(other * 8, 8), 8)],
                dst_ref=gate_recv.at[quarter, pl.ds(pl.multiple_of(me * 8, 8), 8)],
                send_sem=gate_out.at[quarter], recv_sem=gate_in.at[quarter],
                device_id=(other, group), device_id_type=MESH,
            ).start()
            return inner

        lax.fori_loop(1, SEQ, send, 0)
        own = pl.ds(pl.multiple_of(me * 8, 8), 8)
        gate_recv[quarter, own, :] = gate_send[quarter, own, :]
        return carry

    gate_early(0, 0)

    for low in range(2):
        for block in range(8):
            near_send[pl.ds(low * 8 + block, 1), :] = feature(0, 8 + low, block, 1)

    @pl.when((me != 0) & (far_plane != 0) & (far_plane < 5))
    def _():
        near_copy(0).start()

    own_near = pl.ds(pl.multiple_of(me * 32, 32), 32)
    near_recv[own_near, :] = near_send[own_near, :]

    def far_query(block, carry):
        pieces = []
        for low in (0, 2, 1, 3):
            for residue in range(4):
                goal = lax.rem(far_plane + lax.rem(residue - far_plane + 8, 4), 8)
                pieces.append(feature(0, 8 + goal * 32 + low, block, 8, 4))
        turned = jnp.transpose(jnp.concatenate(pieces, axis=0))
        for own in range(2):
            far_send[pl.ds(block * 2 + own, SEQ, 16), :] = turned[own * 64 : own * 64 + 64]
        return carry

    lax.fori_loop(0, 8, far_query, 0)

    def send_far(step, carry):
        other = lax.rem(me + step, SEQ)
        pltpu.make_async_remote_copy(
            src_ref=far_send.at[pl.ds(pl.multiple_of(other * 16, 16), 16)],
            dst_ref=far_recv.at[pl.ds(pl.multiple_of(me * 16, 16), 16)],
            send_sem=far_sems.at[0], recv_sem=far_sems.at[1],
            device_id=(other, group), device_id_type=MESH,
        ).start()
        return carry

    lax.fori_loop(1, SEQ, send_far, 0)
    own_far = pl.ds(pl.multiple_of(me * 16, 16), 16)
    far_recv[own_far, :] = far_send[own_far, :]

    lax.fori_loop(1, QUARTERS, gate_early, 0)

    wait_bytes(filt_recv.at[pl.ds(0, SEQ - 1)], filt_sems.at[1])
    for half in range(2):
        filt_all[group, :, half * LANES : half * LANES + LANES] = filt_recv[:, half, :]

    def send_ring(step, carry):
        other = lax.rem(group + step, GRP)
        pltpu.make_async_remote_copy(
            src_ref=filt_all.at[group], dst_ref=filt_all.at[group],
            send_sem=ring_sems.at[0], recv_sem=ring_sems.at[1],
            device_id=(me, other), device_id_type=MESH,
        ).start()
        return carry

    lax.fori_loop(1, GRP, send_ring, 0)
    for copy in small_loads[2:]:
        copy.wait()

    def spectrum(rows_of):
        reals, imags = [], []
        for f in range(4):
            high, low = halves(rows_of(f))
            coarse = product(head[...], jnp.concatenate([high, low, high], axis=0))
            real, imag = coarse[:SEQ], coarse[SEQ:]
            reals.append(real * twist[0] - imag * twist[1])
            imags.append(real * twist[1] + imag * twist[0])
        both = jnp.concatenate(
            [jnp.concatenate(reals, axis=0), jnp.concatenate(imags, axis=0)], axis=1
        )
        high, low = halves(both)
        return product(high, wide[0]) + product(low, wide[0]) + product(high, wide[1])

    wait_bytes(filt_all.at[pl.ds(0, GRP - 1)], ring_sems.at[1])
    response[...] = spectrum(lambda f: filt_all[f])

    token = lax.broadcasted_iota(jnp.int32, (SEQ, LANES), 0)
    lane = lax.broadcasted_iota(jnp.int32, (SEQ, LANES), 1)
    goal_plane = lane // 64 * 4 + lane % 32 // 8
    is_far = (goal_plane - token // 8 - 2 - token % 2 + 16) % 8 < 4
    is_low = lane < 64

    wait_bytes(far_recv.at[pl.ds(0, (SEQ - 1) * 16)], far_sems.at[1])

    def convolve(quarter, carry):
        wait_bytes(gate_recv.at[quarter, pl.ds(0, (SEQ - 1) * 8)], gate_in.at[quarter])

        def rows_of(f):
            return jnp.concatenate(
                [gate_recv[quarter, pl.ds(f, SEQ, 8), :], gate_recv[quarter, pl.ds(4 + f, SEQ, 8), :]],
                axis=1,
            )

        signal = spectrum(rows_of)
        reals, imags = [], []
        for f in range(4):
            rows = slice(f * SEQ, f * SEQ + SEQ)
            real, imag = signal[rows, :TOK], signal[rows, TOK:]
            skip = gain[(quarter * 4 + f) * SEQ + me]
            tap_real = response[rows, :TOK] + skip
            tap_imag = response[rows, TOK:]
            reals.append(real * tap_real - imag * tap_imag)
            imags.append(real * tap_imag + imag * tap_real)
        both = jnp.concatenate(
            [jnp.concatenate(reals, axis=0), jnp.concatenate(imags, axis=0)], axis=1
        )
        high, low = halves(both)
        back = product(high, wide[2]) + product(low, wide[2]) + product(high, wide[3])
        for f in range(4):
            rows = slice(f * SEQ, f * SEQ + SEQ)
            real, imag = back[rows, :TOK], back[rows, TOK:]
            turned = jnp.concatenate(
                [real * twist[2] - imag * twist[3], real * twist[3] + imag * twist[2]], axis=0
            )
            high, low = halves(turned)
            summed = product(tail[...], jnp.concatenate([high, low, high], axis=0))
            asked = far_recv[pl.ds(quarter * 4 + f, SEQ, 16), :]
            swapped = pltpu.roll(asked, 64, 1)
            first = jnp.where(is_far, jnp.where(is_low, asked, swapped), 1.0)
            second = jnp.where(is_far, jnp.where(is_low, swapped, asked), 1.0)
            stacked = jnp.concatenate(
                [summed[:, :LANES] * first, summed[:, LANES:] * second], axis=0
            )
            flipped = jnp.transpose(stacked)
            for part in range(4):
                start = part // 2 * 256 + part % 2 * 4 + f
                conv_send[quarter, pl.ds(start, 32, 8), :] = flipped[part * 32 : part * 32 + 32]

        def send(step, inner):
            other = lax.rem(me + step, SEQ)
            pltpu.make_async_remote_copy(
                src_ref=conv_send.at[quarter, pl.ds(pl.multiple_of(other * 8, 8), 8)],
                dst_ref=conv_recv.at[quarter, pl.ds(pl.multiple_of(me * 8, 8), 8)],
                send_sem=conv_out.at[quarter], recv_sem=conv_in.at[quarter],
                device_id=(other, group), device_id_type=MESH,
            ).start()
            return inner

        lax.fori_loop(1, SEQ, send, 0)
        own = pl.ds(pl.multiple_of(me * 8, 8), 8)
        conv_recv[quarter, own, :] = conv_send[quarter, own, :]
        return carry

    lax.fori_loop(0, QUARTERS, convolve, 0)

    wait_bytes(near_recv.at[pl.ds(0, 31 * 32)], near_sems.at[1])

    def store(quarter):
        lanes = pl.ds(pl.multiple_of(quarter * 256, 256), 256)
        return pltpu.make_async_copy(
            result.at[:, :, lanes], out_hbm.at[:, :, lanes], out_sem.at[quarter]
        )

    def finish(quarter, carry):
        wait_bytes(conv_recv.at[quarter, pl.ds(0, (SEQ - 1) * 8)], conv_in.at[quarter])
        for pair in range(2):
            block = quarter * 2 + pair
            lanes = pl.ds(pl.multiple_of(block * LANES, LANES), LANES)
            for upper in range(2):
                gathered = jnp.concatenate(
                    [conv_recv[quarter, pl.ds(upper * 4 + pair * 2 + own, SEQ, 8), :] for own in range(2)],
                    axis=0,
                )
                turned = jnp.transpose(gathered)
                for lower in range(2):
                    offset = upper * 2 + lower
                    asked = near_recv[pl.ds(offset * 8 + block, SEQ, 32), :]
                    result[offset, :, lanes] = asked * turned[lower * 64 : lower * 64 + 64]
        store(quarter).start()
        return carry

    lax.fori_loop(0, QUARTERS, finish, 0)

    @pl.when(me < SEQ - 1)
    def _():
        wait_bytes(streams_hbm.at[:, pl.ds(TOK - 8, 8), :], rim_sems.at[0])

    wait_bytes(filt_send.at[pl.ds(0, SEQ - 1)], filt_sems.at[0])
    wait_bytes(filt_all.at[pl.ds(0, GRP - 1)], ring_sems.at[0])
    wait_bytes(near_send.at[pl.ds(0, 31 * 32)], near_sems.at[0])
    wait_bytes(far_send.at[pl.ds(0, (SEQ - 1) * 16)], far_sems.at[0])
    for quarter in range(QUARTERS):
        wait_bytes(gate_send.at[quarter, pl.ds(0, (SEQ - 1) * 8)], gate_out.at[quarter])
        wait_bytes(conv_send.at[quarter, pl.ds(0, (SEQ - 1) * 8)], conv_out.at[quarter])
        store(quarter).wait()


def body(streams, short_filters, skip_gain, long_filter):
    head_all, tail_all, twists, wide = tables()
    dma = pltpu.SemaphoreType.DMA
    f32 = jnp.float32
    in_hbm = pl.BlockSpec(memory_space=pltpu.HBM)
    return pl.pallas_call(
        kernel,
        out_shape=jax.ShapeDtypeStruct((TOK // SEQ, SEQ, CH), f32),
        in_specs=[in_hbm] * 8,
        out_specs=in_hbm,
        scratch_shapes=[
            pltpu.VMEM((3, 8, TOK + 8, LANES), f32),
            pltpu.VMEM((3, 3, CH), f32),
            pltpu.SMEM((CH,), f32),
            pltpu.VMEM((64, TOK), f32),
            pltpu.VMEM(head_all.shape, jnp.bfloat16),
            pltpu.VMEM(tail_all.shape, jnp.bfloat16),
            pltpu.VMEM(twists.shape, f32),
            pltpu.VMEM(wide.shape, jnp.bfloat16),
            pltpu.VMEM((3, 8, 8, LANES), f32),
            pltpu.VMEM((SEQ, 2, LANES), f32),
            pltpu.VMEM((SEQ, 2, LANES), f32),
            pltpu.VMEM((GRP, SEQ, TOK), f32),
            pltpu.VMEM((TOK, 2 * TOK), f32),
            pltpu.VMEM((QUARTERS, SEQ * 8, LANES), f32),
            pltpu.VMEM((QUARTERS, SEQ * 8, LANES), f32),
            pltpu.VMEM((SEQ * 32, LANES), f32),
            pltpu.VMEM((SEQ * 32, LANES), f32),
            pltpu.VMEM((SEQ * 16, LANES), f32),
            pltpu.VMEM((SEQ * 16, LANES), f32),
            pltpu.VMEM((QUARTERS, SEQ * 8, LANES), f32),
            pltpu.VMEM((QUARTERS, SEQ * 8, LANES), f32),
            pltpu.VMEM((TOK // SEQ, SEQ, CH), f32),
            dma((23,)),
            dma((2,)),
            dma((2,)),
            dma((2,)),
            dma((QUARTERS,)),
            dma((QUARTERS,)),
            dma((2,)),
            dma((2,)),
            dma((QUARTERS,)),
            dma((QUARTERS,)),
            dma((QUARTERS,)),
        ],
        compiler_params=pltpu.CompilerParams(
            collective_id=0, has_side_effects=True, vmem_limit_bytes=60 << 20
        ),
    )(streams, short_filters, skip_gain, long_filter.T, head_all, tail_all, twists, wide)


def solution(mesh):
    return jax.shard_map(
        body,
        mesh=mesh,
        in_specs=(P(None, "seq", "grp"), P(None, None, "grp"), P("grp"), P("seq", "grp")),
        out_specs=P("seq", None, "grp"),
        check_vma=False,
    )
```

```python
import functools

import jax
import jax.numpy as jnp
import ml_dtypes
import numpy as np
from jax import lax
from jax.experimental import pallas as pl
from jax.experimental.pallas import tpu as pltpu
from jax.sharding import PartitionSpec as P

MESH = pl.DeviceIdType.MESH
SEQ = 64
GRP = 4
TOK = 256
CH = 1024
POINTS = SEQ * TOK
QUARTERS = 4
LANES = 128


def split_parts(matrix):
    high = matrix.astype(ml_dtypes.bfloat16)
    low = (matrix - high.astype(np.float64)).astype(ml_dtypes.bfloat16)
    return high, low


@functools.cache
def tables():
    r = np.arange(SEQ)
    k1 = np.arange(SEQ)
    m = np.arange(TOK)
    k2 = np.arange(TOK)
    column = np.arange(TOK)
    m_of = 4 * (column // 64 % 2 * 32 + column % 32) + 2 * (column // 32 % 2) + column // 128
    coarse = 2 * np.pi * np.outer(k1 + 0.25, r) / SEQ
    head = np.concatenate([np.cos(coarse), -np.sin(coarse)], axis=0)
    head_high, head_low = split_parts(head)
    head_all = np.concatenate([head_high, head_high, head_low], axis=1)
    tail = np.concatenate([np.cos(coarse.T), -np.sin(coarse.T)], axis=1)
    tail_high, tail_low = split_parts(tail)
    tail_all = np.concatenate([tail_high, tail_high, tail_low], axis=1)
    twist = 2 * np.pi * np.outer(k1 + 0.25, m) / POINTS
    turn = 2 * np.pi * np.outer(k1 + 0.25, m_of) / POINTS
    twists = np.stack(
        [np.cos(twist), -np.sin(twist), np.cos(turn) / POINTS, np.sin(turn) / POINTS]
    ).astype(np.float32)
    fine = 2 * np.pi * (np.outer(m, k2) % TOK) / TOK
    fine_cos, fine_sin = np.cos(fine), -np.sin(fine)
    forward = np.block([[fine_cos, fine_sin], [-fine_sin, fine_cos]])
    back = 2 * np.pi * (np.outer(k2, m_of) % TOK) / TOK
    back_cos, back_sin = np.cos(back), np.sin(back)
    inverse = np.block([[back_cos, back_sin], [-back_sin, back_cos]])
    wide = np.stack([*split_parts(forward), *split_parts(inverse)])
    return head_all, tail_all, twists, wide


def halves(values):
    high = values.astype(jnp.bfloat16)
    low = (values - high.astype(jnp.float32)).astype(jnp.bfloat16)
    return high, low


def product(left, right):
    return jnp.dot(left, right, preferred_element_type=jnp.float32)


def kernel(
    streams_hbm, taps_hbm, gain_hbm, filter_hbm, head_hbm, tail_hbm, twist_hbm, wide_hbm,
    out_ref,
    stream, taps, gain, filt, head, tail, twist, wide,
    rim, filt_send, filt_recv, filt_all, response,
    gate_send, gate_recv, near_send, near_recv, far_send, far_recv, conv_send, conv_recv,
    load_sem, rim_sems, filt_sems, ring_sems, gate_out, gate_in, near_sems, far_sems,
    conv_out, conv_in,
):
    me = lax.axis_index("seq")
    group = lax.axis_index("grp")
    plane, place, side = me // 8, lax.rem(me, 8), lax.rem(me, 2)
    far_plane = lax.rem(plane + 2 + side, 8)
    barrier = pltpu.get_barrier_semaphore()

    def load(source, target, slot):
        return pltpu.make_async_copy(source, target, load_sem.at[slot])

    def query_load(block):
        lanes = pl.ds(block * LANES, LANES)
        return load(streams_hbm.at[0, :, lanes], stream.at[0, block, pl.ds(8, TOK), :], block)

    def gate_load(block):
        lanes = pl.ds(block * LANES, LANES)
        return load(
            streams_hbm.at[pl.ds(1, 2), :, lanes],
            stream.at[pl.ds(1, 2), block, pl.ds(8, TOK), :],
            8 + block,
        )

    small_loads = [
        load(taps_hbm, taps, 16),
        load(filter_hbm, filt, 17),
        load(gain_hbm, gain, 18),
        load(head_hbm, head, 19),
        load(tail_hbm, tail, 20),
        load(twist_hbm, twist, 21),
        load(wide_hbm, wide, 22),
    ]
    small_loads[0].start()
    for block in range(8):
        query_load(block).start()

    def greet(step, carry):
        other = lax.rem(me + step, SEQ)
        pl.semaphore_signal(barrier, inc=1, device_id=(other, group), device_id_type=MESH)
        return carry

    def greet_group(step, carry):
        other = lax.rem(group + step, GRP)
        pl.semaphore_signal(barrier, inc=1, device_id=(me, other), device_id_type=MESH)
        return carry

    lax.fori_loop(1, SEQ, greet, 0)
    lax.fori_loop(1, GRP, greet_group, 0)
    small_loads[1].start()
    for block in range(8):
        gate_load(block).start()
    for copy in small_loads[2:]:
        copy.start()
    for s in range(3):
        stream[s, :, pl.ds(6, 2), :] = jnp.zeros((8, 2, LANES), jnp.float32)

    def wait_bytes(ref, sem):
        pltpu.make_async_copy(ref, ref, sem).wait()

    def feature(s, start, block, size, stride=None):
        lanes = pl.ds(pl.multiple_of(block * LANES, LANES), LANES)

        def rows(first):
            window = pl.ds(first, size) if stride is None else pl.ds(first, size, stride)
            return stream[s, block, window, :]

        return (
            taps[s, 0:1, lanes] * rows(start)
            + taps[s, 1:2, lanes] * rows(start - 1)
            + taps[s, 2:3, lanes] * rows(start - 2)
        )

    small_loads[0].wait()
    for block in range(8):
        query_load(block).wait()

    def near_query(block, carry):
        for step in range(4):
            goal = lax.rem(far_plane + 4 + step, 8)
            for low in range(4):
                featured = feature(0, 8 + goal * 32 + low, block, 8, 4)
                near_send[pl.ds(goal * 256 + low * 8 + block, 8, 32), :] = featured
        return carry

    lax.fori_loop(0, 8, near_query, 0)
    small_loads[1].wait()
    for half in range(2):
        filt_send[:, half, :] = filt[:, half * LANES : half * LANES + LANES]

    pl.semaphore_wait(barrier, SEQ - 1 + GRP - 1)

    def rim_copy(block, other):
        return pltpu.make_async_remote_copy(
            src_ref=streams_hbm.at[:, pl.ds(TOK - 8, 8), pl.ds(block * LANES, LANES)],
            dst_ref=rim.at[:, block], send_sem=rim_sems.at[0], recv_sem=rim_sems.at[1],
            device_id=(other, group), device_id_type=MESH,
        )

    @pl.when(me < SEQ - 1)
    def _():
        for block in range(8):
            rim_copy(block, me + 1).start()

    def near_copy(other):
        return pltpu.make_async_remote_copy(
            src_ref=near_send.at[pl.ds(pl.multiple_of(other * 32, 32), 32)],
            dst_ref=near_recv.at[pl.ds(pl.multiple_of(me * 32, 32), 32)],
            send_sem=near_sems.at[0], recv_sem=near_sems.at[1],
            device_id=(other, group), device_id_type=MESH,
        )

    def send_near(step, carry):
        goal = lax.rem(far_plane + 4 + lax.rem(step, 4), 8)
        other = goal * 8 + lax.rem(place + step // 4, 8)

        @pl.when((other != me) & (other != 0))
        def _():
            near_copy(other).start()

        return carry

    lax.fori_loop(0, 32, send_near, 0)

    def send_filter(step, carry):
        other = lax.rem(me + step, SEQ)
        pltpu.make_async_remote_copy(
            src_ref=filt_send.at[other], dst_ref=filt_recv.at[me],
            send_sem=filt_sems.at[0], recv_sem=filt_sems.at[1],
            device_id=(other, group), device_id_type=MESH,
        ).start()
        return carry

    lax.fori_loop(1, SEQ, send_filter, 0)
    filt_recv[me] = filt_send[me]
    for block in range(8):
        gate_load(block).wait()

    def gate(quarter, half):
        for pair in range(2):
            block = quarter * 2 + pair
            first = 8 + half * LANES
            gated = feature(1, first, block, LANES) * feature(2, first, block, LANES)
            turned = jnp.transpose(gated)
            for own in range(2):
                row = half * 4 + pair * 2 + own
                gate_send[quarter, pl.ds(row, SEQ, 8), :] = turned[own * 64 : own * 64 + 64]

    def gate_late(quarter, carry):
        gate(quarter, 1)
        return carry

    lax.fori_loop(0, QUARTERS, gate_late, 0)

    @pl.when(me > 0)
    def _():
        wait_bytes(rim, rim_sems.at[1])
        for s in range(3):
            stream[s, :, pl.ds(6, 2), :] = rim[s, :, pl.ds(6, 2), :]

    def gate_early(quarter, carry):
        gate(quarter, 0)

        def send(step, inner):
            other = lax.rem(me + step, SEQ)
            pltpu.make_async_remote_copy(
                src_ref=gate_send.at[quarter, pl.ds(pl.multiple_of(other * 8, 8), 8)],
                dst_ref=gate_recv.at[quarter, pl.ds(pl.multiple_of(me * 8, 8), 8)],
                send_sem=gate_out.at[quarter], recv_sem=gate_in.at[quarter],
                device_id=(other, group), device_id_type=MESH,
            ).start()
            return inner

        lax.fori_loop(1, SEQ, send, 0)
        own = pl.ds(pl.multiple_of(me * 8, 8), 8)
        gate_recv[quarter, own, :] = gate_send[quarter, own, :]
        return carry

    gate_early(0, 0)

    for low in range(2):
        for block in range(8):
            near_send[pl.ds(low * 8 + block, 1), :] = feature(0, 8 + low, block, 1)

    @pl.when((me != 0) & (far_plane != 0) & (far_plane < 5))
    def _():
        near_copy(0).start()

    own_near = pl.ds(pl.multiple_of(me * 32, 32), 32)
    near_recv[own_near, :] = near_send[own_near, :]

    def far_query(block, carry):
        pieces = []
        for low in (0, 2, 1, 3):
            for residue in range(4):
                goal = lax.rem(far_plane + lax.rem(residue - far_plane + 8, 4), 8)
                pieces.append(feature(0, 8 + goal * 32 + low, block, 8, 4))
        turned = jnp.transpose(jnp.concatenate(pieces, axis=0))
        for own in range(2):
            far_send[pl.ds(block * 2 + own, SEQ, 16), :] = turned[own * 64 : own * 64 + 64]
        return carry

    lax.fori_loop(0, 8, far_query, 0)

    def send_far(step, carry):
        other = lax.rem(me + step, SEQ)
        pltpu.make_async_remote_copy(
            src_ref=far_send.at[pl.ds(pl.multiple_of(other * 16, 16), 16)],
            dst_ref=far_recv.at[pl.ds(pl.multiple_of(me * 16, 16), 16)],
            send_sem=far_sems.at[0], recv_sem=far_sems.at[1],
            device_id=(other, group), device_id_type=MESH,
        ).start()
        return carry

    lax.fori_loop(1, SEQ, send_far, 0)
    own_far = pl.ds(pl.multiple_of(me * 16, 16), 16)
    far_recv[own_far, :] = far_send[own_far, :]

    lax.fori_loop(1, QUARTERS, gate_early, 0)

    wait_bytes(filt_recv.at[pl.ds(0, SEQ - 1)], filt_sems.at[1])
    for half in range(2):
        filt_all[group, :, half * LANES : half * LANES + LANES] = filt_recv[:, half, :]

    def send_ring(step, carry):
        other = lax.rem(group + step, GRP)
        pltpu.make_async_remote_copy(
            src_ref=filt_all.at[group], dst_ref=filt_all.at[group],
            send_sem=ring_sems.at[0], recv_sem=ring_sems.at[1],
            device_id=(me, other), device_id_type=MESH,
        ).start()
        return carry

    lax.fori_loop(1, GRP, send_ring, 0)
    for copy in small_loads[2:]:
        copy.wait()

    def spectrum(rows_of):
        reals, imags = [], []
        for f in range(4):
            high, low = halves(rows_of(f))
            coarse = product(head[...], jnp.concatenate([high, low, high], axis=0))
            real, imag = coarse[:SEQ], coarse[SEQ:]
            reals.append(real * twist[0] - imag * twist[1])
            imags.append(real * twist[1] + imag * twist[0])
        both = jnp.concatenate(
            [jnp.concatenate(reals, axis=0), jnp.concatenate(imags, axis=0)], axis=1
        )
        high, low = halves(both)
        return product(high, wide[0]) + product(low, wide[0]) + product(high, wide[1])

    wait_bytes(filt_all.at[pl.ds(0, GRP - 1)], ring_sems.at[1])
    response[...] = spectrum(lambda f: filt_all[f])

    token = lax.broadcasted_iota(jnp.int32, (SEQ, LANES), 0)
    lane = lax.broadcasted_iota(jnp.int32, (SEQ, LANES), 1)
    goal_plane = lane // 64 * 4 + lane % 32 // 8
    is_far = (goal_plane - token // 8 - 2 - token % 2 + 16) % 8 < 4
    is_low = lane < 64

    wait_bytes(far_recv.at[pl.ds(0, (SEQ - 1) * 16)], far_sems.at[1])

    def convolve(quarter, carry):
        wait_bytes(gate_recv.at[quarter, pl.ds(0, (SEQ - 1) * 8)], gate_in.at[quarter])

        def rows_of(f):
            return jnp.concatenate(
                [gate_recv[quarter, pl.ds(f, SEQ, 8), :], gate_recv[quarter, pl.ds(4 + f, SEQ, 8), :]],
                axis=1,
            )

        signal = spectrum(rows_of)
        reals, imags = [], []
        for f in range(4):
            rows = slice(f * SEQ, f * SEQ + SEQ)
            real, imag = signal[rows, :TOK], signal[rows, TOK:]
            skip = gain[(quarter * 4 + f) * SEQ + me]
            tap_real = response[rows, :TOK] + skip
            tap_imag = response[rows, TOK:]
            reals.append(real * tap_real - imag * tap_imag)
            imags.append(real * tap_imag + imag * tap_real)
        both = jnp.concatenate(
            [jnp.concatenate(reals, axis=0), jnp.concatenate(imags, axis=0)], axis=1
        )
        high, low = halves(both)
        back = product(high, wide[2]) + product(low, wide[2]) + product(high, wide[3])
        for f in range(4):
            rows = slice(f * SEQ, f * SEQ + SEQ)
            real, imag = back[rows, :TOK], back[rows, TOK:]
            turned = jnp.concatenate(
                [real * twist[2] - imag * twist[3], real * twist[3] + imag * twist[2]], axis=0
            )
            high, low = halves(turned)
            summed = product(tail[...], jnp.concatenate([high, low, high], axis=0))
            asked = far_recv[pl.ds(quarter * 4 + f, SEQ, 16), :]
            swapped = pltpu.roll(asked, 64, 1)
            first = jnp.where(is_far, jnp.where(is_low, asked, swapped), 1.0)
            second = jnp.where(is_far, jnp.where(is_low, swapped, asked), 1.0)
            stacked = jnp.concatenate(
                [summed[:, :LANES] * first, summed[:, LANES:] * second], axis=0
            )
            flipped = jnp.transpose(stacked)
            for part in range(4):
                start = part // 2 * 256 + part % 2 * 4 + f
                conv_send[quarter, pl.ds(start, 32, 8), :] = flipped[part * 32 : part * 32 + 32]

        def send(step, inner):
            other = lax.rem(me + step, SEQ)
            pltpu.make_async_remote_copy(
                src_ref=conv_send.at[quarter, pl.ds(pl.multiple_of(other * 8, 8), 8)],
                dst_ref=conv_recv.at[quarter, pl.ds(pl.multiple_of(me * 8, 8), 8)],
                send_sem=conv_out.at[quarter], recv_sem=conv_in.at[quarter],
                device_id=(other, group), device_id_type=MESH,
            ).start()
            return inner

        lax.fori_loop(1, SEQ, send, 0)
        own = pl.ds(pl.multiple_of(me * 8, 8), 8)
        conv_recv[quarter, own, :] = conv_send[quarter, own, :]
        return carry

    lax.fori_loop(0, QUARTERS, convolve, 0)

    wait_bytes(near_recv.at[pl.ds(0, 31 * 32)], near_sems.at[1])
    came = (plane - token // 8 - 2 - token % 2 + 16) % 8 >= 4

    def stage(block, carry):
        lanes = pl.ds(pl.multiple_of(block * LANES, LANES), LANES)
        for offset in range(4):
            asked = near_recv[pl.ds(offset * 8 + block, SEQ, 32), :]
            out_ref[offset, :, lanes] = jnp.where(came, asked, 1.0)
        return carry

    lax.fori_loop(0, 8, stage, 0)

    def finish(quarter, carry):
        wait_bytes(conv_recv.at[quarter, pl.ds(0, (SEQ - 1) * 8)], conv_in.at[quarter])
        for pair in range(2):
            block = quarter * 2 + pair
            lanes = pl.ds(pl.multiple_of(block * LANES, LANES), LANES)
            for upper in range(2):
                gathered = jnp.concatenate(
                    [conv_recv[quarter, pl.ds(upper * 4 + pair * 2 + own, SEQ, 8), :] for own in range(2)],
                    axis=0,
                )
                turned = jnp.transpose(gathered)
                for lower in range(2):
                    offset = upper * 2 + lower
                    asked = out_ref[offset, :, lanes]
                    out_ref[offset, :, lanes] = asked * turned[lower * 64 : lower * 64 + 64]
        return carry

    lax.fori_loop(0, QUARTERS, finish, 0)

    @pl.when(me < SEQ - 1)
    def _():
        wait_bytes(streams_hbm.at[:, pl.ds(TOK - 8, 8), :], rim_sems.at[0])

    wait_bytes(filt_send.at[pl.ds(0, SEQ - 1)], filt_sems.at[0])
    wait_bytes(filt_all.at[pl.ds(0, GRP - 1)], ring_sems.at[0])
    wait_bytes(near_send.at[pl.ds(0, 31 * 32)], near_sems.at[0])
    wait_bytes(far_send.at[pl.ds(0, (SEQ - 1) * 16)], far_sems.at[0])
    for quarter in range(QUARTERS):
        wait_bytes(gate_send.at[quarter, pl.ds(0, (SEQ - 1) * 8)], gate_out.at[quarter])
        wait_bytes(conv_send.at[quarter, pl.ds(0, (SEQ - 1) * 8)], conv_out.at[quarter])


def body(streams, short_filters, skip_gain, long_filter):
    head_all, tail_all, twists, wide = tables()
    dma = pltpu.SemaphoreType.DMA
    f32 = jnp.float32
    in_hbm = pl.BlockSpec(memory_space=pltpu.HBM)
    return pl.pallas_call(
        kernel,
        out_shape=jax.ShapeDtypeStruct((TOK // SEQ, SEQ, CH), f32),
        in_specs=[in_hbm] * 8,
        out_specs=pl.BlockSpec(memory_space=pltpu.VMEM),
        scratch_shapes=[
            pltpu.VMEM((3, 8, TOK + 8, LANES), f32),
            pltpu.VMEM((3, 3, CH), f32),
            pltpu.SMEM((CH,), f32),
            pltpu.VMEM((64, TOK), f32),
            pltpu.VMEM(head_all.shape, jnp.bfloat16),
            pltpu.VMEM(tail_all.shape, jnp.bfloat16),
            pltpu.VMEM(twists.shape, f32),
            pltpu.VMEM(wide.shape, jnp.bfloat16),
            pltpu.VMEM((3, 8, 8, LANES), f32),
            pltpu.VMEM((SEQ, 2, LANES), f32),
            pltpu.VMEM((SEQ, 2, LANES), f32),
            pltpu.VMEM((GRP, SEQ, TOK), f32),
            pltpu.VMEM((TOK, 2 * TOK), f32),
            pltpu.VMEM((QUARTERS, SEQ * 8, LANES), f32),
            pltpu.VMEM((QUARTERS, SEQ * 8, LANES), f32),
            pltpu.VMEM((SEQ * 32, LANES), f32),
            pltpu.VMEM((SEQ * 32, LANES), f32),
            pltpu.VMEM((SEQ * 16, LANES), f32),
            pltpu.VMEM((SEQ * 16, LANES), f32),
            pltpu.VMEM((QUARTERS, SEQ * 8, LANES), f32),
            pltpu.VMEM((QUARTERS, SEQ * 8, LANES), f32),
            dma((23,)),
            dma((2,)),
            dma((2,)),
            dma((2,)),
            dma((QUARTERS,)),
            dma((QUARTERS,)),
            dma((2,)),
            dma((2,)),
            dma((QUARTERS,)),
            dma((QUARTERS,)),
        ],
        compiler_params=pltpu.CompilerParams(
            collective_id=0, has_side_effects=True, vmem_limit_bytes=48 << 20
        ),
    )(*[pltpu.with_memory_space_constraint(x, pltpu.HBM) for x in (streams, short_filters, skip_gain, long_filter.T, jnp.asarray(head_all), jnp.asarray(tail_all), jnp.asarray(twists), jnp.asarray(wide))])


def solution(mesh):
    return jax.shard_map(
        body,
        mesh=mesh,
        in_specs=(P(None, "seq", "grp"), P(None, None, "grp"), P("grp"), P("seq", "grp")),
        out_specs=P("seq", None, "grp"),
        check_vma=False,
    )
```

```python
import functools

import jax
import jax.numpy as jnp
import ml_dtypes
import numpy as np
from jax import lax
from jax.experimental import pallas as pl
from jax.experimental.pallas import tpu as pltpu
from jax.sharding import PartitionSpec as P

MESH = pl.DeviceIdType.MESH
SEQ = 64
GRP = 4
TOK = 256
CH = 1024
POINTS = SEQ * TOK
QUARTERS = 4
LANES = 128


def split_parts(matrix):
    high = matrix.astype(ml_dtypes.bfloat16)
    low = (matrix - high.astype(np.float64)).astype(ml_dtypes.bfloat16)
    return high, low


@functools.cache
def tables():
    r = np.arange(SEQ)
    k1 = np.arange(SEQ)
    m = np.arange(TOK)
    k2 = np.arange(TOK)
    column = np.arange(TOK)
    m_of = 4 * (column // 64 % 2 * 32 + column % 32) + 2 * (column // 32 % 2) + column // 128
    coarse = 2 * np.pi * np.outer(k1 + 0.25, r) / SEQ
    head = np.concatenate([np.cos(coarse), -np.sin(coarse)], axis=0)
    head_high, head_low = split_parts(head)
    head_all = np.concatenate([head_high, head_high, head_low], axis=1)
    tail = np.concatenate([np.cos(coarse.T), -np.sin(coarse.T)], axis=1)
    tail_high, tail_low = split_parts(tail)
    tail_all = np.concatenate([tail_high, tail_high, tail_low], axis=1)
    twist = 2 * np.pi * np.outer(k1 + 0.25, m) / POINTS
    turn = 2 * np.pi * np.outer(k1 + 0.25, m_of) / POINTS
    twists = np.stack(
        [np.cos(twist), -np.sin(twist), np.cos(turn) / POINTS, np.sin(turn) / POINTS]
    ).astype(np.float32)
    fine = 2 * np.pi * (np.outer(m, k2) % TOK) / TOK
    fine_cos, fine_sin = np.cos(fine), -np.sin(fine)
    forward = np.block([[fine_cos, fine_sin], [-fine_sin, fine_cos]])
    back = 2 * np.pi * (np.outer(k2, m_of) % TOK) / TOK
    back_cos, back_sin = np.cos(back), np.sin(back)
    inverse = np.block([[back_cos, back_sin], [-back_sin, back_cos]])
    wide = np.stack([*split_parts(forward), *split_parts(inverse)])
    return head_all, tail_all, twists, wide


def halves(values):
    high = values.astype(jnp.bfloat16)
    low = (values - high.astype(jnp.float32)).astype(jnp.bfloat16)
    return high, low


def product(left, right):
    return jnp.dot(left, right, preferred_element_type=jnp.float32)


def kernel(
    streams_hbm, taps_hbm, gain_hbm, filter_hbm, head_hbm, tail_hbm, twist_hbm, wide_hbm,
    out_ref,
    stream, taps, gain, filt, head, tail, twist, wide,
    rim, filt_send, filt_recv, filt_all, response,
    gate_send, gate_recv, near_send, near_recv, far_send, far_recv, anti_send, anti_recv,
    own_send, own_recv, conv_send, conv_recv,
    load_sem, rim_sems, filt_sems, ring_sems, gate_out, gate_in, near_sems, far_sems, anti_sems, own_sems,
    conv_out, conv_in,
):
    me = lax.axis_index("seq")
    group = lax.axis_index("grp")
    plane, place, side = me // 8, lax.rem(me, 8), lax.rem(me, 2)
    far_plane = lax.rem(plane + 2 + side, 8)
    opposite = lax.rem(plane + 4, 8)
    barrier = pltpu.get_barrier_semaphore()

    def load(source, target, slot):
        return pltpu.make_async_copy(source, target, load_sem.at[slot])

    def query_load(block):
        lanes = pl.ds(block * LANES, LANES)
        return load(streams_hbm.at[0, :, lanes], stream.at[0, block, pl.ds(8, TOK), :], block)

    def gate_load(block):
        lanes = pl.ds(block * LANES, LANES)
        return load(
            streams_hbm.at[pl.ds(1, 2), :, lanes],
            stream.at[pl.ds(1, 2), block, pl.ds(8, TOK), :],
            8 + block,
        )

    small_loads = [
        load(taps_hbm, taps, 16),
        load(filter_hbm, filt, 17),
        load(gain_hbm, gain, 18),
        load(head_hbm, head, 19),
        load(tail_hbm, tail, 20),
        load(twist_hbm, twist, 21),
        load(wide_hbm, wide, 22),
    ]
    small_loads[0].start()
    for block in range(8):
        query_load(block).start()

    def greet(step, carry):
        other = lax.rem(me + step, SEQ)
        pl.semaphore_signal(barrier, inc=1, device_id=(other, group), device_id_type=MESH)
        return carry

    def greet_group(step, carry):
        other = lax.rem(group + step, GRP)
        pl.semaphore_signal(barrier, inc=1, device_id=(me, other), device_id_type=MESH)
        return carry

    lax.fori_loop(1, SEQ, greet, 0)
    lax.fori_loop(1, GRP, greet_group, 0)
    small_loads[1].start()
    for block in range(8):
        gate_load(block).start()
    for copy in small_loads[2:]:
        copy.start()
    for s in range(3):
        stream[s, :, pl.ds(6, 2), :] = jnp.zeros((8, 2, LANES), jnp.float32)

    def wait_bytes(ref, sem):
        pltpu.make_async_copy(ref, ref, sem).wait()

    def feature(s, start, block, size, stride=None):
        lanes = pl.ds(pl.multiple_of(block * LANES, LANES), LANES)

        def rows(first):
            window = pl.ds(first, size) if stride is None else pl.ds(first, size, stride)
            return stream[s, block, window, :]

        return (
            taps[s, 0:1, lanes] * rows(start)
            + taps[s, 1:2, lanes] * rows(start - 1)
            + taps[s, 2:3, lanes] * rows(start - 2)
        )

    small_loads[0].wait()
    for block in range(8):
        query_load(block).wait()

    def packed_query(start, size, stride, low, rows):
        owned = lax.broadcasted_iota(jnp.int32, (size, LANES), 1) % 64 // 8 == plane
        last = feature(0, start, 7, size, stride)
        for block in range(7):
            shift = lax.rem(plane - lax.rem(plane + 1 + block, 8) + 16, 16) * 8
            moved = pltpu.roll(last, shift, 1)
            near_send[rows, block, low, :] = jnp.where(
                owned, moved, feature(0, start, block, size, stride)
            )

    def near_query(step, carry):
        goal = lax.rem(far_plane + 4 + step, 8)
        for low in range(4):
            packed_query(8 + goal * 32 + low, 8, 4, low, pl.ds(goal * 8, 8))
        return carry

    lax.fori_loop(0, 4, near_query, 0)
    small_loads[1].wait()
    for half in range(2):
        filt_send[:, half, :] = filt[:, half * LANES : half * LANES + LANES]

    pl.semaphore_wait(barrier, SEQ - 1 + GRP - 1)

    def rim_copy(block, other):
        return pltpu.make_async_remote_copy(
            src_ref=streams_hbm.at[:, pl.ds(TOK - 8, 8), pl.ds(block * LANES, LANES)],
            dst_ref=rim.at[:, block], send_sem=rim_sems.at[0], recv_sem=rim_sems.at[1],
            device_id=(other, group), device_id_type=MESH,
        )

    @pl.when(me < SEQ - 1)
    def _():
        for block in range(8):
            rim_copy(block, me + 1).start()

    def near_copy(other):
        return pltpu.make_async_remote_copy(
            src_ref=near_send.at[other], dst_ref=near_recv.at[me],
            send_sem=near_sems.at[0], recv_sem=near_sems.at[1],
            device_id=(other, group), device_id_type=MESH,
        )

    def send_near(step, carry):
        goal = lax.rem(far_plane + 4 + lax.rem(step, 4), 8)
        other = goal * 8 + lax.rem(place + step // 4, 8)

        @pl.when((other != me) & (other != 0))
        def _():
            near_copy(other).start()

        return carry

    lax.fori_loop(0, 32, send_near, 0)

    def send_filter(step, carry):
        other = lax.rem(me + step, SEQ)
        pltpu.make_async_remote_copy(
            src_ref=filt_send.at[other], dst_ref=filt_recv.at[me],
            send_sem=filt_sems.at[0], recv_sem=filt_sems.at[1],
            device_id=(other, group), device_id_type=MESH,
        ).start()
        return carry

    lax.fori_loop(1, SEQ, send_filter, 0)
    filt_recv[me] = filt_send[me]
    for block in range(8):
        gate_load(block).wait()

    def gate(quarter, half):
        for pair in range(2):
            block = quarter * 2 + pair
            first = 8 + half * LANES
            gated = feature(1, first, block, LANES) * feature(2, first, block, LANES)
            turned = jnp.transpose(gated)
            for own in range(2):
                row = half * 4 + pair * 2 + own
                gate_send[quarter, pl.ds(row, SEQ, 8), :] = turned[own * 64 : own * 64 + 64]

    def gate_late(quarter, carry):
        gate(quarter, 1)
        return carry

    lax.fori_loop(0, QUARTERS, gate_late, 0)

    @pl.when(me > 0)
    def _():
        wait_bytes(rim, rim_sems.at[1])
        for s in range(3):
            stream[s, :, pl.ds(6, 2), :] = rim[s, :, pl.ds(6, 2), :]

    def gate_early(quarter, carry):
        gate(quarter, 0)

        def send(step, inner):
            other = lax.rem(me + step, SEQ)
            pltpu.make_async_remote_copy(
                src_ref=gate_send.at[quarter, pl.ds(pl.multiple_of(other * 8, 8), 8)],
                dst_ref=gate_recv.at[quarter, pl.ds(pl.multiple_of(me * 8, 8), 8)],
                send_sem=gate_out.at[quarter], recv_sem=gate_in.at[quarter],
                device_id=(other, group), device_id_type=MESH,
            ).start()
            return inner

        lax.fori_loop(1, SEQ, send, 0)
        own = pl.ds(pl.multiple_of(me * 8, 8), 8)
        gate_recv[quarter, own, :] = gate_send[quarter, own, :]
        return carry

    gate_early(0, 0)

    for low in range(2):
        packed_query(8 + low, 1, None, low, pl.ds(0, 1))

    @pl.when((me != 0) & (far_plane != 0) & (far_plane < 5))
    def _():
        near_copy(0).start()

    near_recv[me] = near_send[me]

    def turned_query(block, first, target):
        pieces = []
        for low in (0, 2, 1, 3):
            for residue in range(4):
                goal = lax.rem(first + lax.rem(residue - far_plane + 8, 4), 8)
                pieces.append(feature(0, 8 + goal * 32 + low, block, 8, 4))
        turned = jnp.transpose(jnp.concatenate(pieces, axis=0))
        for own in range(2):
            target[pl.ds(block * 2 + own, SEQ, 16), :] = turned[own * 64 : own * 64 + 64]

    def far_query(block, carry):
        turned_query(block, far_plane, far_send)
        return carry

    lax.fori_loop(0, 8, far_query, 0)

    def send_far(step, carry):
        other = lax.rem(me + step, SEQ)

        @pl.when(other // 8 != opposite)
        def _():
            pltpu.make_async_remote_copy(
                src_ref=far_send.at[pl.ds(pl.multiple_of(other * 16, 16), 16)],
                dst_ref=far_recv.at[pl.ds(pl.multiple_of(me * 16, 16), 16)],
                send_sem=far_sems.at[0], recv_sem=far_sems.at[1],
                device_id=(other, group), device_id_type=MESH,
            ).start()

        return carry

    lax.fori_loop(1, SEQ, send_far, 0)
    own_far = pl.ds(pl.multiple_of(me * 16, 16), 16)
    far_recv[own_far, :] = far_send[own_far, :]

    slab = [far_send[pl.ds(opposite * 128 + i, 8, 16), :] for i in range(16)]
    turned = jnp.transpose(jnp.concatenate(slab, axis=0))
    for low in range(4):
        anti_send[:, low, :] = turned[low * 32 : low * 32 + 32]

    def send_anti(step, carry):
        residue = lax.rem(step, 4)
        goal = lax.rem(far_plane + lax.rem(residue - far_plane + 8, 4), 8)
        spot = lax.rem(place + step // 4, 8)
        pltpu.make_async_remote_copy(
            src_ref=anti_send.at[residue * 8 + spot], dst_ref=anti_recv.at[me],
            send_sem=anti_sems.at[0], recv_sem=anti_sems.at[1],
            device_id=(goal * 8 + spot, group), device_id_type=MESH,
        ).start()
        return carry

    lax.fori_loop(0, 32, send_anti, 0)

    lax.fori_loop(1, QUARTERS, gate_early, 0)

    def own_query(block, carry):
        turned_query(block, far_plane + 4, own_send)
        return carry

    lax.fori_loop(0, 8, own_query, 0)

    def send_own(step, carry):
        other = plane * 8 + lax.rem(place + step, 8)
        pltpu.make_async_remote_copy(
            src_ref=own_send.at[pl.ds(pl.multiple_of(other * 16, 16), 16)],
            dst_ref=own_recv.at[pl.ds(pl.multiple_of(me * 16, 16), 16)],
            send_sem=own_sems.at[0], recv_sem=own_sems.at[1],
            device_id=(other, group), device_id_type=MESH,
        ).start()
        return carry

    lax.fori_loop(1, 8, send_own, 0)
    own_recv[own_far, :] = own_send[own_far, :]

    wait_bytes(filt_recv.at[pl.ds(0, SEQ - 1)], filt_sems.at[1])
    for half in range(2):
        filt_all[group, :, half * LANES : half * LANES + LANES] = filt_recv[:, half, :]

    def send_ring(step, carry):
        other = lax.rem(group + step, GRP)
        pltpu.make_async_remote_copy(
            src_ref=filt_all.at[group], dst_ref=filt_all.at[group],
            send_sem=ring_sems.at[0], recv_sem=ring_sems.at[1],
            device_id=(me, other), device_id_type=MESH,
        ).start()
        return carry

    lax.fori_loop(1, GRP, send_ring, 0)
    for copy in small_loads[2:]:
        copy.wait()

    def spectrum(rows_of):
        reals, imags = [], []
        for f in range(4):
            high, low = halves(rows_of(f))
            coarse = product(head[...], jnp.concatenate([high, low, high], axis=0))
            real, imag = coarse[:SEQ], coarse[SEQ:]
            reals.append(real * twist[0] - imag * twist[1])
            imags.append(real * twist[1] + imag * twist[0])
        both = jnp.concatenate(
            [jnp.concatenate(reals, axis=0), jnp.concatenate(imags, axis=0)], axis=1
        )
        high, low = halves(both)
        return product(high, wide[0]) + product(low, wide[0]) + product(high, wide[1])

    wait_bytes(filt_all.at[pl.ds(0, GRP - 1)], ring_sems.at[1])
    response[...] = spectrum(lambda f: filt_all[f])

    token = lax.broadcasted_iota(jnp.int32, (SEQ, LANES), 0)
    lane = lax.broadcasted_iota(jnp.int32, (SEQ, LANES), 1)
    goal_plane = lane // 64 * 4 + lane % 32 // 8
    is_far = (goal_plane - token // 8 - 2 - token % 2 + 16) % 8 < 4
    is_own = jnp.logical_not(is_far) & (token // 8 == plane)
    is_far = is_far & ((token // 8 - plane + 8) % 8 != 4)
    is_low = lane < 64

    wait_bytes(far_recv.at[pl.ds(0, (SEQ - 9) * 16)], far_sems.at[1])
    wait_bytes(own_recv.at[pl.ds(0, 7 * 16)], own_sems.at[1])

    def convolve(quarter, carry):
        wait_bytes(gate_recv.at[quarter, pl.ds(0, (SEQ - 1) * 8)], gate_in.at[quarter])

        def rows_of(f):
            return jnp.concatenate(
                [gate_recv[quarter, pl.ds(f, SEQ, 8), :], gate_recv[quarter, pl.ds(4 + f, SEQ, 8), :]],
                axis=1,
            )

        signal = spectrum(rows_of)
        reals, imags = [], []
        for f in range(4):
            rows = slice(f * SEQ, f * SEQ + SEQ)
            real, imag = signal[rows, :TOK], signal[rows, TOK:]
            skip = gain[(quarter * 4 + f) * SEQ + me]
            tap_real = response[rows, :TOK] + skip
            tap_imag = response[rows, TOK:]
            reals.append(real * tap_real - imag * tap_imag)
            imags.append(real * tap_imag + imag * tap_real)
        both = jnp.concatenate(
            [jnp.concatenate(reals, axis=0), jnp.concatenate(imags, axis=0)], axis=1
        )
        high, low = halves(both)
        back = product(high, wide[2]) + product(low, wide[2]) + product(high, wide[3])
        for f in range(4):
            rows = slice(f * SEQ, f * SEQ + SEQ)
            real, imag = back[rows, :TOK], back[rows, TOK:]
            turned = jnp.concatenate(
                [real * twist[2] - imag * twist[3], real * twist[3] + imag * twist[2]], axis=0
            )
            high, low = halves(turned)
            summed = product(tail[...], jnp.concatenate([high, low, high], axis=0))
            asked = far_recv[pl.ds(quarter * 4 + f, SEQ, 16), :]
            swapped = pltpu.roll(asked, 64, 1)
            mine = own_recv[pl.ds(quarter * 4 + f, SEQ, 16), :]
            crossed_mine = pltpu.roll(mine, 64, 1)
            first = jnp.where(is_own, jnp.where(is_low, mine, crossed_mine), 1.0)
            second = jnp.where(is_own, jnp.where(is_low, crossed_mine, mine), 1.0)
            first = jnp.where(is_far, jnp.where(is_low, asked, swapped), first)
            second = jnp.where(is_far, jnp.where(is_low, swapped, asked), second)
            stacked = jnp.concatenate(
                [summed[:, :LANES] * first, summed[:, LANES:] * second], axis=0
            )
            flipped = jnp.transpose(stacked)
            for part in range(4):
                start = part // 2 * 256 + part % 2 * 4 + f
                conv_send[quarter, pl.ds(start, 32, 8), :] = flipped[part * 32 : part * 32 + 32]

        def send(step, inner):
            other = lax.rem(me + step, SEQ)
            pltpu.make_async_remote_copy(
                src_ref=conv_send.at[quarter, pl.ds(pl.multiple_of(other * 8, 8), 8)],
                dst_ref=conv_recv.at[quarter, pl.ds(pl.multiple_of(me * 8, 8), 8)],
                send_sem=conv_out.at[quarter], recv_sem=conv_in.at[quarter],
                device_id=(other, group), device_id_type=MESH,
            ).start()
            return inner

        lax.fori_loop(1, SEQ, send, 0)
        own = pl.ds(pl.multiple_of(me * 8, 8), 8)
        conv_recv[quarter, own, :] = conv_send[quarter, own, :]
        return carry

    lax.fori_loop(0, QUARTERS, convolve, 0)

    wait_bytes(near_recv.at[pl.ds(0, 31)], near_sems.at[1])
    came = (plane - token // 8 - 2 - token % 2 + 16) % 8 >= 4
    wait_bytes(anti_recv.at[pl.ds(0, 32)], anti_sems.at[1])
    crossed = lane % 64 // 8 == (token // 8 + 4) % 8

    lane_plane = lane % 64 // 8
    apart = lane_plane != token // 8

    def far_factor(block, offset):
        packed = anti_recv[:, offset % 2 * 2 + offset // 2, :]
        firsts, seconds = [], []
        for z in range(8):
            rows = packed[z * 8 : z * 8 + 8]
            shift = (z + 4) % 8 * 8 + 128 - 16 * block
            firsts.append(pltpu.roll(rows, lax.rem(shift, LANES), 1))
            seconds.append(pltpu.roll(rows, lax.rem(shift + 56, LANES), 1))
        opened = jnp.where(
            is_low, jnp.concatenate(firsts, axis=0), jnp.concatenate(seconds, axis=0)
        )
        return jnp.where(crossed, opened, 1.0)

    def stage(block, carry):
        lanes = pl.ds(pl.multiple_of(block * LANES, LANES), LANES)
        for offset in range(4):
            asked = jnp.where(apart, near_recv[:, block, offset, :], 1.0)
            out_ref[offset, :, lanes] = jnp.where(came, asked, far_factor(block, offset))
        return carry

    lax.fori_loop(0, 7, stage, 0)
    for offset in range(4):
        gathered = jnp.ones((SEQ, LANES), jnp.float32)
        for block in range(7):
            source = near_recv[:, block, offset, :]
            pieces = []
            for z in range(8):
                shift = ((z + 1 + block) % 8 - z) * 8 % LANES
                pieces.append(pltpu.roll(source[z * 8 : z * 8 + 8], shift, 1))
            here = lane_plane == (token // 8 + 1 + block) % 8
            gathered = jnp.where(here, jnp.concatenate(pieces, axis=0), gathered)
        out_ref[offset, :, pl.ds(7 * LANES, LANES)] = jnp.where(
            came, gathered, far_factor(7, offset)
        )

    def finish(quarter, carry):
        wait_bytes(conv_recv.at[quarter, pl.ds(0, (SEQ - 1) * 8)], conv_in.at[quarter])
        for pair in range(2):
            block = quarter * 2 + pair
            lanes = pl.ds(pl.multiple_of(block * LANES, LANES), LANES)
            for upper in range(2):
                gathered = jnp.concatenate(
                    [conv_recv[quarter, pl.ds(upper * 4 + pair * 2 + own, SEQ, 8), :] for own in range(2)],
                    axis=0,
                )
                turned = jnp.transpose(gathered)
                for lower in range(2):
                    offset = upper * 2 + lower
                    asked = out_ref[offset, :, lanes]
                    out_ref[offset, :, lanes] = asked * turned[lower * 64 : lower * 64 + 64]
        return carry

    lax.fori_loop(0, QUARTERS, finish, 0)

    @pl.when(me < SEQ - 1)
    def _():
        wait_bytes(streams_hbm.at[:, pl.ds(TOK - 8, 8), :], rim_sems.at[0])

    wait_bytes(filt_send.at[pl.ds(0, SEQ - 1)], filt_sems.at[0])
    wait_bytes(filt_all.at[pl.ds(0, GRP - 1)], ring_sems.at[0])
    wait_bytes(near_send.at[pl.ds(0, 31)], near_sems.at[0])
    wait_bytes(own_send.at[pl.ds(0, 7 * 16)], own_sems.at[0])
    wait_bytes(far_send.at[pl.ds(0, (SEQ - 9) * 16)], far_sems.at[0])
    wait_bytes(anti_send, anti_sems.at[0])
    for quarter in range(QUARTERS):
        wait_bytes(gate_send.at[quarter, pl.ds(0, (SEQ - 1) * 8)], gate_out.at[quarter])
        wait_bytes(conv_send.at[quarter, pl.ds(0, (SEQ - 1) * 8)], conv_out.at[quarter])


def body(streams, short_filters, skip_gain, long_filter):
    head_all, tail_all, twists, wide = tables()
    dma = pltpu.SemaphoreType.DMA
    f32 = jnp.float32
    in_hbm = pl.BlockSpec(memory_space=pltpu.HBM)
    return pl.pallas_call(
        kernel,
        out_shape=jax.ShapeDtypeStruct((TOK // SEQ, SEQ, CH), f32),
        in_specs=[in_hbm] * 8,
        out_specs=pl.BlockSpec(memory_space=pltpu.VMEM),
        scratch_shapes=[
            pltpu.VMEM((3, 8, TOK + 8, LANES), f32),
            pltpu.VMEM((3, 3, CH), f32),
            pltpu.SMEM((CH,), f32),
            pltpu.VMEM((64, TOK), f32),
            pltpu.VMEM(head_all.shape, jnp.bfloat16),
            pltpu.VMEM(tail_all.shape, jnp.bfloat16),
            pltpu.VMEM(twists.shape, f32),
            pltpu.VMEM(wide.shape, jnp.bfloat16),
            pltpu.VMEM((3, 8, 8, LANES), f32),
            pltpu.VMEM((SEQ, 2, LANES), f32),
            pltpu.VMEM((SEQ, 2, LANES), f32),
            pltpu.VMEM((GRP, SEQ, TOK), f32),
            pltpu.VMEM((TOK, 2 * TOK), f32),
            pltpu.VMEM((QUARTERS, SEQ * 8, LANES), f32),
            pltpu.VMEM((QUARTERS, SEQ * 8, LANES), f32),
            pltpu.VMEM((SEQ, 7, 4, LANES), f32),
            pltpu.VMEM((SEQ, 7, 4, LANES), f32),
            pltpu.VMEM((SEQ * 16, LANES), f32),
            pltpu.VMEM((SEQ * 16, LANES), f32),
            pltpu.VMEM((32, 4, LANES), f32),
            pltpu.VMEM((SEQ, 4, LANES), f32),
            pltpu.VMEM((SEQ * 16, LANES), f32),
            pltpu.VMEM((SEQ * 16, LANES), f32),
            pltpu.VMEM((QUARTERS, SEQ * 8, LANES), f32),
            pltpu.VMEM((QUARTERS, SEQ * 8, LANES), f32),
            dma((23,)),
            dma((2,)),
            dma((2,)),
            dma((2,)),
            dma((QUARTERS,)),
            dma((QUARTERS,)),
            dma((2,)),
            dma((2,)),
            dma((2,)),
            dma((2,)),
            dma((QUARTERS,)),
            dma((QUARTERS,)),
        ],
        compiler_params=pltpu.CompilerParams(
            collective_id=0, has_side_effects=True, vmem_limit_bytes=48 << 20
        ),
    )(*[pltpu.with_memory_space_constraint(x, pltpu.HBM) for x in (streams, short_filters, skip_gain, long_filter.T, jnp.asarray(head_all), jnp.asarray(tail_all), jnp.asarray(twists), jnp.asarray(wide))])


def solution(mesh):
    return jax.shard_map(
        body,
        mesh=mesh,
        in_specs=(P(None, "seq", "grp"), P(None, None, "grp"), P("grp"), P("seq", "grp")),
        out_specs=P("seq", None, "grp"),
        check_vma=False,
    )
```

```python
import functools

import jax
import jax.numpy as jnp
import ml_dtypes
import numpy as np
from jax import lax
from jax.experimental import pallas as pl
from jax.experimental.pallas import tpu as pltpu
from jax.sharding import PartitionSpec as P

MESH = pl.DeviceIdType.MESH
SEQ = 64
GRP = 4
TOK = 256
CH = 1024
POINTS = SEQ * TOK
QUARTERS = 4
LANES = 128


def split_parts(matrix):
    high = matrix.astype(ml_dtypes.bfloat16)
    low = (matrix - high.astype(np.float64)).astype(ml_dtypes.bfloat16)
    return high, low


@functools.cache
def tables():
    r = np.arange(SEQ)
    k1 = np.arange(SEQ)
    m = np.arange(TOK)
    k2 = np.arange(TOK)
    column = np.arange(TOK)
    m_of = 4 * (column // 64 % 2 * 32 + column % 32) + 2 * (column // 32 % 2) + column // 128
    coarse = 2 * np.pi * np.outer(k1 + 0.25, r) / SEQ
    head = np.concatenate([np.cos(coarse), -np.sin(coarse)], axis=0)
    head_high, head_low = split_parts(head)
    head_all = np.concatenate([head_high, head_high, head_low], axis=1)
    tail = np.concatenate([np.cos(coarse.T), -np.sin(coarse.T)], axis=1)
    tail_high, tail_low = split_parts(tail)
    tail_all = np.concatenate([tail_high, tail_high, tail_low], axis=1)
    twist = 2 * np.pi * np.outer(k1 + 0.25, m) / POINTS
    turn = 2 * np.pi * np.outer(k1 + 0.25, m_of) / POINTS
    twists = np.stack(
        [np.cos(twist), -np.sin(twist), np.cos(turn) / POINTS, np.sin(turn) / POINTS]
    ).astype(np.float32)
    fine = 2 * np.pi * (np.outer(m, k2) % TOK) / TOK
    fine_cos, fine_sin = np.cos(fine), -np.sin(fine)
    forward = np.block([[fine_cos, fine_sin], [-fine_sin, fine_cos]])
    back = 2 * np.pi * (np.outer(k2, m_of) % TOK) / TOK
    back_cos, back_sin = np.cos(back), np.sin(back)
    inverse = np.block([[back_cos, back_sin], [-back_sin, back_cos]])
    wide = np.stack([*split_parts(forward), *split_parts(inverse)])
    return head_all, tail_all, twists, wide


def halves(values):
    high = values.astype(jnp.bfloat16)
    low = (values - high.astype(jnp.float32)).astype(jnp.bfloat16)
    return high, low


def product(left, right):
    return jnp.dot(left, right, preferred_element_type=jnp.float32)


def kernel(
    streams_hbm, taps_hbm, gain_hbm, filter_hbm, head_hbm, tail_hbm, twist_hbm, wide_hbm,
    out_ref,
    stream, taps, gain, filt, head, tail, twist, wide,
    ends, rim_send, rim, filt_send, filt_recv, filt_all, response,
    gate_send, gate_recv, near_send, near_recv, far_send, far_recv, anti_send, anti_recv,
    own_send, own_recv, conv_send, conv_recv,
    load_sem, rim_sems, filt_sems, ring_sems, gate_out, gate_in, near_sems, far_sems, anti_sems, own_sems,
    conv_out, conv_in,
):
    me = lax.axis_index("seq")
    group = lax.axis_index("grp")
    plane, place, side = me // 8, lax.rem(me, 8), lax.rem(me, 2)
    far_plane = lax.rem(plane + 2 + side, 8)
    opposite = lax.rem(plane + 4, 8)
    barrier = pltpu.get_barrier_semaphore()

    def load(source, target, slot):
        return pltpu.make_async_copy(source, target, load_sem.at[slot])

    def query_load(block):
        lanes = pl.ds(block * LANES, LANES)
        return load(streams_hbm.at[0, :, lanes], stream.at[0, block, pl.ds(8, TOK), :], block)

    def gate_load(block):
        lanes = pl.ds(block * LANES, LANES)
        return load(
            streams_hbm.at[pl.ds(1, 2), :, lanes],
            stream.at[pl.ds(1, 2), block, pl.ds(8, TOK), :],
            8 + block,
        )

    small_loads = [
        load(taps_hbm, taps, 16),
        load(filter_hbm, filt, 17),
        load(gain_hbm, gain, 18),
        load(head_hbm, head, 19),
        load(tail_hbm, tail, 20),
        load(twist_hbm, twist, 21),
        load(wide_hbm, wide, 22),
    ]
    small_loads[0].start()
    for block in range(8):
        query_load(block).start()
    for block in range(8):
        last_rows = streams_hbm.at[:, pl.ds(TOK - 8, 8), pl.ds(block * LANES, LANES)]
        load(last_rows, ends.at[:, block], 23).start()

    def greet(step, carry):
        other = lax.rem(me + step, SEQ)
        pl.semaphore_signal(barrier, inc=1, device_id=(other, group), device_id_type=MESH)
        return carry

    def greet_group(step, carry):
        other = lax.rem(group + step, GRP)
        pl.semaphore_signal(barrier, inc=1, device_id=(me, other), device_id_type=MESH)
        return carry

    lax.fori_loop(1, SEQ, greet, 0)
    lax.fori_loop(1, GRP, greet_group, 0)
    small_loads[1].start()
    for block in range(8):
        gate_load(block).start()
    for copy in small_loads[2:]:
        copy.start()
    for s in range(3):
        stream[s, :, pl.ds(6, 2), :] = jnp.zeros((8, 2, LANES), jnp.float32)

    def wait_bytes(ref, sem):
        pltpu.make_async_copy(ref, ref, sem).wait()

    def feature(s, start, block, size, stride=None):
        lanes = pl.ds(pl.multiple_of(block * LANES, LANES), LANES)

        def rows(first):
            window = pl.ds(first, size) if stride is None else pl.ds(first, size, stride)
            return stream[s, block, window, :]

        return (
            taps[s, 0:1, lanes] * rows(start)
            + taps[s, 1:2, lanes] * rows(start - 1)
            + taps[s, 2:3, lanes] * rows(start - 2)
        )

    small_loads[0].wait()
    for block in range(8):
        query_load(block).wait()

    def packed_query(start, size, stride, low, rows):
        owned = lax.broadcasted_iota(jnp.int32, (size, LANES), 1) % 64 // 8 == plane
        last = feature(0, start, 7, size, stride)
        for block in range(7):
            shift = lax.rem(plane - lax.rem(plane + 1 + block, 8) + 16, 16) * 8
            moved = pltpu.roll(last, shift, 1)
            near_send[rows, block, low, :] = jnp.where(
                owned, moved, feature(0, start, block, size, stride)
            )

    def near_query(step, carry):
        goal = lax.rem(far_plane + 4 + step, 8)
        for low in range(4):
            packed_query(8 + goal * 32 + low, 8, 4, low, pl.ds(goal * 8, 8))
        return carry

    lax.fori_loop(0, 4, near_query, 0)
    small_loads[1].wait()
    for half in range(2):
        filt_send[:, half, :] = filt[:, half * LANES : half * LANES + LANES]

    wait_bytes(ends, load_sem.at[23])
    rim_send[...] = ends[:, :, 6:8, :]
    pl.semaphore_wait(barrier, SEQ - 1 + GRP - 1)

    @pl.when(me < SEQ - 1)
    def _():
        pltpu.make_async_remote_copy(
            src_ref=rim_send, dst_ref=rim, send_sem=rim_sems.at[0], recv_sem=rim_sems.at[1],
            device_id=(me + 1, group), device_id_type=MESH,
        ).start()

    def near_copy(other):
        return pltpu.make_async_remote_copy(
            src_ref=near_send.at[other], dst_ref=near_recv.at[me],
            send_sem=near_sems.at[0], recv_sem=near_sems.at[1],
            device_id=(other, group), device_id_type=MESH,
        )

    def send_near(step, carry):
        goal = lax.rem(far_plane + 4 + lax.rem(step, 4), 8)
        other = goal * 8 + lax.rem(place + step // 4, 8)

        @pl.when((other != me) & (other != 0))
        def _():
            near_copy(other).start()

        return carry

    lax.fori_loop(0, 32, send_near, 0)

    def send_filter(step, carry):
        other = lax.rem(me + step, SEQ)
        pltpu.make_async_remote_copy(
            src_ref=filt_send.at[other], dst_ref=filt_recv.at[me],
            send_sem=filt_sems.at[0], recv_sem=filt_sems.at[1],
            device_id=(other, group), device_id_type=MESH,
        ).start()
        return carry

    lax.fori_loop(1, SEQ, send_filter, 0)
    filt_recv[me] = filt_send[me]
    for block in range(8):
        gate_load(block).wait()

    def gate(quarter, half):
        for pair in range(2):
            block = quarter * 2 + pair
            first = 8 + half * LANES
            gated = feature(1, first, block, LANES) * feature(2, first, block, LANES)
            turned = jnp.transpose(gated)
            for own in range(2):
                row = half * 4 + pair * 2 + own
                gate_send[quarter, pl.ds(row, SEQ, 8), :] = turned[own * 64 : own * 64 + 64]

    def gate_late(quarter, carry):
        gate(quarter, 1)
        return carry

    lax.fori_loop(0, QUARTERS, gate_late, 0)

    @pl.when(me > 0)
    def _():
        wait_bytes(rim, rim_sems.at[1])
        for s in range(3):
            stream[s, :, pl.ds(6, 2), :] = rim[s]

    def gate_early(quarter, carry):
        gate(quarter, 0)

        def send(step, inner):
            other = lax.rem(me + step, SEQ)
            pltpu.make_async_remote_copy(
                src_ref=gate_send.at[quarter, pl.ds(pl.multiple_of(other * 8, 8), 8)],
                dst_ref=gate_recv.at[quarter, pl.ds(pl.multiple_of(me * 8, 8), 8)],
                send_sem=gate_out.at[quarter], recv_sem=gate_in.at[quarter],
                device_id=(other, group), device_id_type=MESH,
            ).start()
            return inner

        lax.fori_loop(1, SEQ, send, 0)
        own = pl.ds(pl.multiple_of(me * 8, 8), 8)
        gate_recv[quarter, own, :] = gate_send[quarter, own, :]
        return carry

    gate_early(0, 0)

    for low in range(2):
        packed_query(8 + low, 1, None, low, pl.ds(0, 1))

    @pl.when((me != 0) & (far_plane != 0) & (far_plane < 5))
    def _():
        near_copy(0).start()

    near_recv[me] = near_send[me]

    def turned_query(block, first, target):
        pieces = []
        for low in (0, 2, 1, 3):
            for residue in range(4):
                goal = lax.rem(first + lax.rem(residue - far_plane + 8, 4), 8)
                pieces.append(feature(0, 8 + goal * 32 + low, block, 8, 4))
        turned = jnp.transpose(jnp.concatenate(pieces, axis=0))
        for own in range(2):
            target[pl.ds(block * 2 + own, SEQ, 16), :] = turned[own * 64 : own * 64 + 64]

    def far_query(block, carry):
        turned_query(block, far_plane, far_send)
        return carry

    lax.fori_loop(0, 8, far_query, 0)

    def send_far(step, carry):
        other = lax.rem(me + step, SEQ)

        @pl.when(other // 8 != opposite)
        def _():
            pltpu.make_async_remote_copy(
                src_ref=far_send.at[pl.ds(pl.multiple_of(other * 16, 16), 16)],
                dst_ref=far_recv.at[pl.ds(pl.multiple_of(me * 16, 16), 16)],
                send_sem=far_sems.at[0], recv_sem=far_sems.at[1],
                device_id=(other, group), device_id_type=MESH,
            ).start()

        return carry

    lax.fori_loop(1, SEQ, send_far, 0)
    own_far = pl.ds(pl.multiple_of(me * 16, 16), 16)
    far_recv[own_far, :] = far_send[own_far, :]

    slab = [far_send[pl.ds(opposite * 128 + i, 8, 16), :] for i in range(16)]
    turned = jnp.transpose(jnp.concatenate(slab, axis=0))
    for low in range(4):
        anti_send[:, low, :] = turned[low * 32 : low * 32 + 32]

    def send_anti(step, carry):
        residue = lax.rem(step, 4)
        goal = lax.rem(far_plane + lax.rem(residue - far_plane + 8, 4), 8)
        spot = lax.rem(place + step // 4, 8)
        pltpu.make_async_remote_copy(
            src_ref=anti_send.at[residue * 8 + spot], dst_ref=anti_recv.at[me],
            send_sem=anti_sems.at[0], recv_sem=anti_sems.at[1],
            device_id=(goal * 8 + spot, group), device_id_type=MESH,
        ).start()
        return carry

    lax.fori_loop(0, 32, send_anti, 0)

    lax.fori_loop(1, QUARTERS, gate_early, 0)

    def own_query(block, carry):
        turned_query(block, far_plane + 4, own_send)
        return carry

    lax.fori_loop(0, 8, own_query, 0)

    def send_own(step, carry):
        other = plane * 8 + lax.rem(place + step, 8)
        pltpu.make_async_remote_copy(
            src_ref=own_send.at[pl.ds(pl.multiple_of(other * 16, 16), 16)],
            dst_ref=own_recv.at[pl.ds(pl.multiple_of(me * 16, 16), 16)],
            send_sem=own_sems.at[0], recv_sem=own_sems.at[1],
            device_id=(other, group), device_id_type=MESH,
        ).start()
        return carry

    lax.fori_loop(1, 8, send_own, 0)
    own_recv[own_far, :] = own_send[own_far, :]

    wait_bytes(filt_recv.at[pl.ds(0, SEQ - 1)], filt_sems.at[1])
    for half in range(2):
        filt_all[group, :, half * LANES : half * LANES + LANES] = filt_recv[:, half, :]

    def send_ring(step, carry):
        other = lax.rem(group + step, GRP)
        pltpu.make_async_remote_copy(
            src_ref=filt_all.at[group], dst_ref=filt_all.at[group],
            send_sem=ring_sems.at[0], recv_sem=ring_sems.at[1],
            device_id=(me, other), device_id_type=MESH,
        ).start()
        return carry

    lax.fori_loop(1, GRP, send_ring, 0)
    for copy in small_loads[2:]:
        copy.wait()

    def spectrum(rows_of):
        reals, imags = [], []
        for f in range(4):
            high, low = halves(rows_of(f))
            coarse = product(head[...], jnp.concatenate([high, low, high], axis=0))
            real, imag = coarse[:SEQ], coarse[SEQ:]
            reals.append(real * twist[0] - imag * twist[1])
            imags.append(real * twist[1] + imag * twist[0])
        both = jnp.concatenate(
            [jnp.concatenate(reals, axis=0), jnp.concatenate(imags, axis=0)], axis=1
        )
        high, low = halves(both)
        return product(high, wide[0]) + product(low, wide[0]) + product(high, wide[1])

    wait_bytes(filt_all.at[pl.ds(0, GRP - 1)], ring_sems.at[1])
    response[...] = spectrum(lambda f: filt_all[f])

    token = lax.broadcasted_iota(jnp.int32, (SEQ, LANES), 0)
    lane = lax.broadcasted_iota(jnp.int32, (SEQ, LANES), 1)
    goal_plane = lane // 64 * 4 + lane % 32 // 8
    is_far = (goal_plane - token // 8 - 2 - token % 2 + 16) % 8 < 4
    is_own = jnp.logical_not(is_far) & (token // 8 == plane)
    is_far = is_far & ((token // 8 - plane + 8) % 8 != 4)
    is_low = lane < 64

    wait_bytes(far_recv.at[pl.ds(0, (SEQ - 9) * 16)], far_sems.at[1])
    wait_bytes(own_recv.at[pl.ds(0, 7 * 16)], own_sems.at[1])

    def convolve(quarter, carry):
        wait_bytes(gate_recv.at[quarter, pl.ds(0, (SEQ - 1) * 8)], gate_in.at[quarter])

        def rows_of(f):
            return jnp.concatenate(
                [gate_recv[quarter, pl.ds(f, SEQ, 8), :], gate_recv[quarter, pl.ds(4 + f, SEQ, 8), :]],
                axis=1,
            )

        signal = spectrum(rows_of)
        reals, imags = [], []
        for f in range(4):
            rows = slice(f * SEQ, f * SEQ + SEQ)
            real, imag = signal[rows, :TOK], signal[rows, TOK:]
            skip = gain[(quarter * 4 + f) * SEQ + me]
            tap_real = response[rows, :TOK] + skip
            tap_imag = response[rows, TOK:]
            reals.append(real * tap_real - imag * tap_imag)
            imags.append(real * tap_imag + imag * tap_real)
        both = jnp.concatenate(
            [jnp.concatenate(reals, axis=0), jnp.concatenate(imags, axis=0)], axis=1
        )
        high, low = halves(both)
        back = product(high, wide[2]) + product(low, wide[2]) + product(high, wide[3])
        for f in range(4):
            rows = slice(f * SEQ, f * SEQ + SEQ)
            real, imag = back[rows, :TOK], back[rows, TOK:]
            turned = jnp.concatenate(
                [real * twist[2] - imag * twist[3], real * twist[3] + imag * twist[2]], axis=0
            )
            high, low = halves(turned)
            summed = product(tail[...], jnp.concatenate([high, low, high], axis=0))
            asked = far_recv[pl.ds(quarter * 4 + f, SEQ, 16), :]
            swapped = pltpu.roll(asked, 64, 1)
            mine = own_recv[pl.ds(quarter * 4 + f, SEQ, 16), :]
            crossed_mine = pltpu.roll(mine, 64, 1)
            first = jnp.where(is_own, jnp.where(is_low, mine, crossed_mine), 1.0)
            second = jnp.where(is_own, jnp.where(is_low, crossed_mine, mine), 1.0)
            first = jnp.where(is_far, jnp.where(is_low, asked, swapped), first)
            second = jnp.where(is_far, jnp.where(is_low, swapped, asked), second)
            stacked = jnp.concatenate(
                [summed[:, :LANES] * first, summed[:, LANES:] * second], axis=0
            )
            flipped = jnp.transpose(stacked)
            for part in range(4):
                start = part // 2 * 256 + part % 2 * 4 + f
                conv_send[quarter, pl.ds(start, 32, 8), :] = flipped[part * 32 : part * 32 + 32]

        def send(step, inner):
            other = lax.rem(me + step, SEQ)
            pltpu.make_async_remote_copy(
                src_ref=conv_send.at[quarter, pl.ds(pl.multiple_of(other * 8, 8), 8)],
                dst_ref=conv_recv.at[quarter, pl.ds(pl.multiple_of(me * 8, 8), 8)],
                send_sem=conv_out.at[quarter], recv_sem=conv_in.at[quarter],
                device_id=(other, group), device_id_type=MESH,
            ).start()
            return inner

        lax.fori_loop(1, SEQ, send, 0)
        own = pl.ds(pl.multiple_of(me * 8, 8), 8)
        conv_recv[quarter, own, :] = conv_send[quarter, own, :]
        return carry

    lax.fori_loop(0, QUARTERS, convolve, 0)

    wait_bytes(near_recv.at[pl.ds(0, 31)], near_sems.at[1])
    came = (plane - token // 8 - 2 - token % 2 + 16) % 8 >= 4
    wait_bytes(anti_recv.at[pl.ds(0, 32)], anti_sems.at[1])
    crossed = lane % 64 // 8 == (token // 8 + 4) % 8

    lane_plane = lane % 64 // 8
    apart = lane_plane != token // 8

    def far_factor(block, offset):
        packed = anti_recv[:, offset % 2 * 2 + offset // 2, :]
        firsts, seconds = [], []
        for z in range(8):
            rows = packed[z * 8 : z * 8 + 8]
            shift = (z + 4) % 8 * 8 + 128 - 16 * block
            firsts.append(pltpu.roll(rows, lax.rem(shift, LANES), 1))
            seconds.append(pltpu.roll(rows, lax.rem(shift + 56, LANES), 1))
        opened = jnp.where(
            is_low, jnp.concatenate(firsts, axis=0), jnp.concatenate(seconds, axis=0)
        )
        return jnp.where(crossed, opened, 1.0)

    def stage(block, carry):
        lanes = pl.ds(pl.multiple_of(block * LANES, LANES), LANES)
        for offset in range(4):
            asked = jnp.where(apart, near_recv[:, block, offset, :], 1.0)
            out_ref[offset, :, lanes] = jnp.where(came, asked, far_factor(block, offset))
        return carry

    lax.fori_loop(0, 7, stage, 0)
    for offset in range(4):
        gathered = jnp.ones((SEQ, LANES), jnp.float32)
        for block in range(7):
            source = near_recv[:, block, offset, :]
            pieces = []
            for z in range(8):
                shift = ((z + 1 + block) % 8 - z) * 8 % LANES
                pieces.append(pltpu.roll(source[z * 8 : z * 8 + 8], shift, 1))
            here = lane_plane == (token // 8 + 1 + block) % 8
            gathered = jnp.where(here, jnp.concatenate(pieces, axis=0), gathered)
        out_ref[offset, :, pl.ds(7 * LANES, LANES)] = jnp.where(
            came, gathered, far_factor(7, offset)
        )

    def finish(quarter, carry):
        wait_bytes(conv_recv.at[quarter, pl.ds(0, (SEQ - 1) * 8)], conv_in.at[quarter])
        for pair in range(2):
            block = quarter * 2 + pair
            lanes = pl.ds(pl.multiple_of(block * LANES, LANES), LANES)
            for upper in range(2):
                gathered = jnp.concatenate(
                    [conv_recv[quarter, pl.ds(upper * 4 + pair * 2 + own, SEQ, 8), :] for own in range(2)],
                    axis=0,
                )
                turned = jnp.transpose(gathered)
                for lower in range(2):
                    offset = upper * 2 + lower
                    asked = out_ref[offset, :, lanes]
                    out_ref[offset, :, lanes] = asked * turned[lower * 64 : lower * 64 + 64]
        return carry

    lax.fori_loop(0, QUARTERS, finish, 0)

    @pl.when(me < SEQ - 1)
    def _():
        wait_bytes(rim_send, rim_sems.at[0])

    wait_bytes(filt_send.at[pl.ds(0, SEQ - 1)], filt_sems.at[0])
    wait_bytes(filt_all.at[pl.ds(0, GRP - 1)], ring_sems.at[0])
    wait_bytes(near_send.at[pl.ds(0, 31)], near_sems.at[0])
    wait_bytes(own_send.at[pl.ds(0, 7 * 16)], own_sems.at[0])
    wait_bytes(far_send.at[pl.ds(0, (SEQ - 9) * 16)], far_sems.at[0])
    wait_bytes(anti_send, anti_sems.at[0])
    for quarter in range(QUARTERS):
        wait_bytes(gate_send.at[quarter, pl.ds(0, (SEQ - 1) * 8)], gate_out.at[quarter])
        wait_bytes(conv_send.at[quarter, pl.ds(0, (SEQ - 1) * 8)], conv_out.at[quarter])


def body(streams, short_filters, skip_gain, long_filter):
    head_all, tail_all, twists, wide = tables()
    dma = pltpu.SemaphoreType.DMA
    f32 = jnp.float32
    in_hbm = pl.BlockSpec(memory_space=pltpu.HBM)
    return pl.pallas_call(
        kernel,
        out_shape=jax.ShapeDtypeStruct((TOK // SEQ, SEQ, CH), f32),
        in_specs=[in_hbm] * 8,
        out_specs=pl.BlockSpec(memory_space=pltpu.VMEM),
        scratch_shapes=[
            pltpu.VMEM((3, 8, TOK + 8, LANES), f32),
            pltpu.VMEM((3, 3, CH), f32),
            pltpu.SMEM((CH,), f32),
            pltpu.VMEM((64, TOK), f32),
            pltpu.VMEM(head_all.shape, jnp.bfloat16),
            pltpu.VMEM(tail_all.shape, jnp.bfloat16),
            pltpu.VMEM(twists.shape, f32),
            pltpu.VMEM(wide.shape, jnp.bfloat16),
            pltpu.VMEM((3, 8, 8, LANES), f32),
            pltpu.VMEM((3, 8, 2, LANES), f32),
            pltpu.VMEM((3, 8, 2, LANES), f32),
            pltpu.VMEM((SEQ, 2, LANES), f32),
            pltpu.VMEM((SEQ, 2, LANES), f32),
            pltpu.VMEM((GRP, SEQ, TOK), f32),
            pltpu.VMEM((TOK, 2 * TOK), f32),
            pltpu.VMEM((QUARTERS, SEQ * 8, LANES), f32),
            pltpu.VMEM((QUARTERS, SEQ * 8, LANES), f32),
            pltpu.VMEM((SEQ, 7, 4, LANES), f32),
            pltpu.VMEM((SEQ, 7, 4, LANES), f32),
            pltpu.VMEM((SEQ * 16, LANES), f32),
            pltpu.VMEM((SEQ * 16, LANES), f32),
            pltpu.VMEM((32, 4, LANES), f32),
            pltpu.VMEM((SEQ, 4, LANES), f32),
            pltpu.VMEM((SEQ * 16, LANES), f32),
            pltpu.VMEM((SEQ * 16, LANES), f32),
            pltpu.VMEM((QUARTERS, SEQ * 8, LANES), f32),
            pltpu.VMEM((QUARTERS, SEQ * 8, LANES), f32),
            dma((24,)),
            dma((2,)),
            dma((2,)),
            dma((2,)),
            dma((QUARTERS,)),
            dma((QUARTERS,)),
            dma((2,)),
            dma((2,)),
            dma((2,)),
            dma((2,)),
            dma((QUARTERS,)),
            dma((QUARTERS,)),
        ],
        compiler_params=pltpu.CompilerParams(
            collective_id=0, has_side_effects=True, vmem_limit_bytes=48 << 20
        ),
    )(*[pltpu.with_memory_space_constraint(x, pltpu.HBM) for x in (streams, short_filters, skip_gain, long_filter.T, jnp.asarray(head_all), jnp.asarray(tail_all), jnp.asarray(twists), jnp.asarray(wide))])


def solution(mesh):
    return jax.shard_map(
        body,
        mesh=mesh,
        in_specs=(P(None, "seq", "grp"), P(None, None, "grp"), P("grp"), P("seq", "grp")),
        out_specs=P("seq", None, "grp"),
        check_vma=False,
    )
```

```python
import functools

import jax
import jax.numpy as jnp
import ml_dtypes
import numpy as np
from jax import lax
from jax.experimental import pallas as pl
from jax.experimental.pallas import tpu as pltpu
from jax.sharding import PartitionSpec as P

MESH = pl.DeviceIdType.MESH
SEQ = 64
GRP = 4
TOK = 256
CH = 1024
POINTS = SEQ * TOK
QUARTERS = 4
LANES = 128


def split_parts(matrix):
    high = matrix.astype(ml_dtypes.bfloat16)
    low = (matrix - high.astype(np.float64)).astype(ml_dtypes.bfloat16)
    return high, low


@functools.cache
def tables():
    r = np.arange(SEQ)
    k1 = np.arange(SEQ)
    m = np.arange(TOK)
    k2 = np.arange(TOK)
    column = np.arange(TOK)
    m_of = 4 * (column // 64 % 2 * 32 + column % 32) + 2 * (column // 32 % 2) + column // 128
    coarse = 2 * np.pi * np.outer(k1 + 0.25, r) / SEQ
    head = np.concatenate([np.cos(coarse), -np.sin(coarse)], axis=0)
    head_high, head_low = split_parts(head)
    head_all = np.concatenate([head_high, head_high, head_low], axis=1)
    tail = np.concatenate([np.cos(coarse.T), -np.sin(coarse.T)], axis=1)
    tail_high, tail_low = split_parts(tail)
    tail_all = np.concatenate([tail_high, tail_high, tail_low], axis=1)
    twist = 2 * np.pi * np.outer(k1 + 0.25, m) / POINTS
    turn = 2 * np.pi * np.outer(k1 + 0.25, m_of) / POINTS
    twists = np.stack(
        [np.cos(twist), -np.sin(twist), np.cos(turn) / POINTS, np.sin(turn) / POINTS]
    ).astype(np.float32)
    fine = 2 * np.pi * (np.outer(m, k2) % TOK) / TOK
    fine_cos, fine_sin = np.cos(fine), -np.sin(fine)
    forward = np.block([[fine_cos, fine_sin], [-fine_sin, fine_cos]])
    back = 2 * np.pi * (np.outer(k2, m_of) % TOK) / TOK
    back_cos, back_sin = np.cos(back), np.sin(back)
    inverse = np.block([[back_cos, back_sin], [-back_sin, back_cos]])
    wide = np.stack([*split_parts(forward), *split_parts(inverse)])
    return head_all, tail_all, twists, wide


def halves(values):
    high = values.astype(jnp.bfloat16)
    low = (values - high.astype(jnp.float32)).astype(jnp.bfloat16)
    return high, low


def product(left, right):
    return jnp.dot(left, right, preferred_element_type=jnp.float32)


def kernel(
    streams_hbm, taps_hbm, gain_hbm, filter_hbm, head_hbm, tail_hbm, twist_hbm, wide_hbm,
    out_ref,
    stream, taps, gain, filt, head, tail, twist, wide,
    ends, rim_send, rim, filt_send, filt_recv, filt_all, response,
    gate_send, gate_recv, near_send, near_recv, far_send, far_recv, anti_send, anti_recv,
    own_send, own_recv, conv_send, conv_recv,
    load_sem, rim_sems, filt_sems, ring_sems, gate_out, gate_in, near_sems, far_sems, anti_sems, own_sems,
    conv_out, conv_in,
):
    me = lax.axis_index("seq")
    group = lax.axis_index("grp")
    plane, place, side = me // 8, lax.rem(me, 8), lax.rem(me, 2)
    far_plane = lax.rem(plane + 2 + side, 8)
    opposite = lax.rem(plane + 4, 8)
    barrier = pltpu.get_barrier_semaphore()

    def load(source, target, slot):
        return pltpu.make_async_copy(source, target, load_sem.at[slot])

    def query_load(block):
        lanes = pl.ds(block * LANES, LANES)
        return load(streams_hbm.at[0, :, lanes], stream.at[0, block, pl.ds(8, TOK), :], block)

    def gate_load(block):
        lanes = pl.ds(block * LANES, LANES)
        return load(
            streams_hbm.at[pl.ds(1, 2), :, lanes],
            stream.at[pl.ds(1, 2), block, pl.ds(8, TOK), :],
            8 + block,
        )

    small_loads = [
        load(taps_hbm, taps, 16),
        load(filter_hbm, filt, 17),
        load(gain_hbm, gain, 18),
        load(head_hbm, head, 19),
        load(tail_hbm, tail, 20),
        load(twist_hbm, twist, 21),
        load(wide_hbm, wide, 22),
    ]
    small_loads[0].start()
    for block in range(8):
        query_load(block).start()
    for block in range(8):
        last_rows = streams_hbm.at[:, pl.ds(TOK - 8, 8), pl.ds(block * LANES, LANES)]
        load(last_rows, ends.at[:, block], 23).start()

    def greet(step, carry):
        other = lax.rem(me + step, SEQ)
        pl.semaphore_signal(barrier, inc=1, device_id=(other, group), device_id_type=MESH)
        return carry

    def greet_group(step, carry):
        other = lax.rem(group + step, GRP)
        pl.semaphore_signal(barrier, inc=1, device_id=(me, other), device_id_type=MESH)
        return carry

    lax.fori_loop(1, SEQ, greet, 0)
    lax.fori_loop(1, GRP, greet_group, 0)
    small_loads[1].start()
    for block in range(8):
        gate_load(block).start()
    for copy in small_loads[2:]:
        copy.start()
    for s in range(3):
        stream[s, :, pl.ds(6, 2), :] = jnp.zeros((8, 2, LANES), jnp.float32)

    def wait_bytes(ref, sem):
        pltpu.make_async_copy(ref, ref, sem).wait()

    def feature(s, start, block, size, stride=None):
        lanes = pl.ds(pl.multiple_of(block * LANES, LANES), LANES)

        def rows(first):
            window = pl.ds(first, size) if stride is None else pl.ds(first, size, stride)
            return stream[s, block, window, :]

        return (
            taps[s, 0:1, lanes] * rows(start)
            + taps[s, 1:2, lanes] * rows(start - 1)
            + taps[s, 2:3, lanes] * rows(start - 2)
        )

    small_loads[0].wait()
    for block in range(8):
        query_load(block).wait()

    def packed_query(start, size, stride, low, rows):
        owned = lax.broadcasted_iota(jnp.int32, (size, LANES), 1) % 64 // 8 == plane
        last = feature(0, start, 7, size, stride)
        for block in range(7):
            shift = lax.rem(plane - lax.rem(plane + 1 + block, 8) + 16, 16) * 8
            moved = pltpu.roll(last, shift, 1)
            near_send[rows, block, low, :] = jnp.where(
                owned, moved, feature(0, start, block, size, stride)
            )

    def near_query(step, carry):
        goal = lax.rem(far_plane + 4 + step, 8)
        for low in range(4):
            packed_query(8 + goal * 32 + low, 8, 4, low, pl.ds(goal * 8, 8))
        return carry

    lax.fori_loop(0, 4, near_query, 0)
    small_loads[1].wait()
    for half in range(2):
        filt_send[:, half, :] = filt[:, half * LANES : half * LANES + LANES]

    wait_bytes(ends, load_sem.at[23])
    rim_send[...] = ends[:, :, 6:8, :]
    pl.semaphore_wait(barrier, SEQ - 1 + GRP - 1)

    @pl.when(me < SEQ - 1)
    def _():
        pltpu.make_async_remote_copy(
            src_ref=rim_send, dst_ref=rim, send_sem=rim_sems.at[0], recv_sem=rim_sems.at[1],
            device_id=(me + 1, group), device_id_type=MESH,
        ).start()

    def near_copy(other):
        return pltpu.make_async_remote_copy(
            src_ref=near_send.at[other], dst_ref=near_recv.at[me],
            send_sem=near_sems.at[0], recv_sem=near_sems.at[1],
            device_id=(other, group), device_id_type=MESH,
        )

    def send_near(step, carry):
        goal = lax.rem(far_plane + 4 + lax.rem(step, 4), 8)
        other = goal * 8 + lax.rem(place + step // 4, 8)

        @pl.when((other != me) & (other != 0))
        def _():
            near_copy(other).start()

        return carry

    lax.fori_loop(0, 32, send_near, 0)

    def send_filter(step, carry):
        other = lax.rem(me + step, SEQ)
        pltpu.make_async_remote_copy(
            src_ref=filt_send.at[other], dst_ref=filt_recv.at[me],
            send_sem=filt_sems.at[0], recv_sem=filt_sems.at[1],
            device_id=(other, group), device_id_type=MESH,
        ).start()
        return carry

    lax.fori_loop(1, SEQ, send_filter, 0)
    filt_recv[me] = filt_send[me]
    for block in range(8):
        gate_load(block).wait()

    def gate(quarter, half):
        for pair in range(2):
            block = quarter * 2 + pair
            first = 8 + half * LANES
            gated = feature(1, first, block, LANES) * feature(2, first, block, LANES)
            turned = jnp.transpose(gated)
            for own in range(2):
                row = half * 4 + pair * 2 + own
                gate_send[quarter, pl.ds(row, SEQ, 8), :] = turned[own * 64 : own * 64 + 64]

    def gate_late(quarter, carry):
        gate(quarter, 1)
        return carry

    lax.fori_loop(0, QUARTERS, gate_late, 0)

    @pl.when(me > 0)
    def _():
        wait_bytes(rim, rim_sems.at[1])
        for s in range(3):
            stream[s, :, pl.ds(6, 2), :] = rim[s]

    def gate_early(quarter, carry):
        gate(quarter, 0)

        def send(step, inner):
            other = lax.rem(me + step, SEQ)
            pltpu.make_async_remote_copy(
                src_ref=gate_send.at[quarter, pl.ds(pl.multiple_of(other * 8, 8), 8)],
                dst_ref=gate_recv.at[quarter, pl.ds(pl.multiple_of(me * 8, 8), 8)],
                send_sem=gate_out.at[quarter], recv_sem=gate_in.at[quarter],
                device_id=(other, group), device_id_type=MESH,
            ).start()
            return inner

        lax.fori_loop(1, SEQ, send, 0)
        own = pl.ds(pl.multiple_of(me * 8, 8), 8)
        gate_recv[quarter, own, :] = gate_send[quarter, own, :]
        return carry

    gate_early(0, 0)

    for low in range(2):
        packed_query(8 + low, 1, None, low, pl.ds(0, 1))

    @pl.when((me != 0) & (far_plane != 0) & (far_plane < 5))
    def _():
        near_copy(0).start()

    near_recv[me] = near_send[me]

    def turned_query(block, first, target):
        pieces = []
        for low in (0, 2, 1, 3):
            for residue in range(4):
                goal = lax.rem(first + lax.rem(residue - far_plane + 8, 4), 8)
                pieces.append(feature(0, 8 + goal * 32 + low, block, 8, 4))
        turned = jnp.transpose(jnp.concatenate(pieces, axis=0))
        for own in range(2):
            target[pl.ds(block * 2 + own, SEQ, 16), :] = turned[own * 64 : own * 64 + 64]

    def far_query(block, carry):
        turned_query(block, far_plane, far_send)
        return carry

    lax.fori_loop(0, 8, far_query, 0)

    def send_far(step, carry):
        other = lax.rem(me + step, SEQ)

        @pl.when(other // 8 != opposite)
        def _():
            pltpu.make_async_remote_copy(
                src_ref=far_send.at[pl.ds(pl.multiple_of(other * 16, 16), 16)],
                dst_ref=far_recv.at[pl.ds(pl.multiple_of(me * 16, 16), 16)],
                send_sem=far_sems.at[0], recv_sem=far_sems.at[1],
                device_id=(other, group), device_id_type=MESH,
            ).start()

        return carry

    lax.fori_loop(1, SEQ, send_far, 0)
    own_far = pl.ds(pl.multiple_of(me * 16, 16), 16)
    far_recv[own_far, :] = far_send[own_far, :]

    slab = [far_send[pl.ds(opposite * 128 + i, 8, 16), :] for i in range(16)]
    turned = jnp.transpose(jnp.concatenate(slab, axis=0))
    for low in range(4):
        anti_send[:, low, :] = turned[low * 32 : low * 32 + 32]

    def send_anti(step, carry):
        residue = lax.rem(step, 4)
        goal = lax.rem(far_plane + lax.rem(residue - far_plane + 8, 4), 8)
        spot = lax.rem(place + step // 4, 8)
        pltpu.make_async_remote_copy(
            src_ref=anti_send.at[residue * 8 + spot], dst_ref=anti_recv.at[me],
            send_sem=anti_sems.at[0], recv_sem=anti_sems.at[1],
            device_id=(goal * 8 + spot, group), device_id_type=MESH,
        ).start()
        return carry

    lax.fori_loop(0, 32, send_anti, 0)

    lax.fori_loop(1, QUARTERS, gate_early, 0)

    def own_query(block, carry):
        turned_query(block, far_plane + 4, own_send)
        return carry

    lax.fori_loop(0, 8, own_query, 0)

    def send_own(step, carry):
        other = plane * 8 + lax.rem(place + step, 8)
        pltpu.make_async_remote_copy(
            src_ref=own_send.at[pl.ds(pl.multiple_of(other * 16, 16), 16)],
            dst_ref=own_recv.at[pl.ds(pl.multiple_of(me * 16, 16), 16)],
            send_sem=own_sems.at[0], recv_sem=own_sems.at[1],
            device_id=(other, group), device_id_type=MESH,
        ).start()
        return carry

    lax.fori_loop(1, 8, send_own, 0)
    own_recv[own_far, :] = own_send[own_far, :]

    wait_bytes(filt_recv.at[pl.ds(0, SEQ - 1)], filt_sems.at[1])
    for half in range(2):
        filt_all[group, :, half * LANES : half * LANES + LANES] = filt_recv[:, half, :]

    def send_ring(step, carry):
        other = lax.rem(group + step, GRP)
        pltpu.make_async_remote_copy(
            src_ref=filt_all.at[group], dst_ref=filt_all.at[group],
            send_sem=ring_sems.at[0], recv_sem=ring_sems.at[1],
            device_id=(me, other), device_id_type=MESH,
        ).start()
        return carry

    lax.fori_loop(1, GRP, send_ring, 0)
    for copy in small_loads[2:]:
        copy.wait()

    def spectrum(rows_of):
        reals, imags = [], []
        for f in range(4):
            high, low = halves(rows_of(f))
            coarse = product(head[...], jnp.concatenate([high, low, high], axis=0))
            real, imag = coarse[:SEQ], coarse[SEQ:]
            reals.append(real * twist[0] - imag * twist[1])
            imags.append(real * twist[1] + imag * twist[0])
        both = jnp.concatenate(
            [jnp.concatenate(reals, axis=0), jnp.concatenate(imags, axis=0)], axis=1
        )
        high, low = halves(both)
        return product(high, wide[0]) + product(low, wide[0]) + product(high, wide[1])

    wait_bytes(filt_all.at[pl.ds(0, GRP - 1)], ring_sems.at[1])
    response[...] = spectrum(lambda f: filt_all[f])

    token = lax.broadcasted_iota(jnp.int32, (SEQ, LANES), 0)
    lane = lax.broadcasted_iota(jnp.int32, (SEQ, LANES), 1)
    goal_plane = lane // 64 * 4 + lane % 32 // 8
    is_far = (goal_plane - token // 8 - 2 - token % 2 + 16) % 8 < 4
    is_own = jnp.logical_not(is_far) & (token // 8 == plane)
    is_far = is_far & ((token // 8 - plane + 8) % 8 != 4)
    is_low = lane < 64

    wait_bytes(far_recv.at[pl.ds(0, (SEQ - 9) * 16)], far_sems.at[1])
    wait_bytes(own_recv.at[pl.ds(0, 7 * 16)], own_sems.at[1])

    def convolve(quarter, carry):
        wait_bytes(gate_recv.at[quarter, pl.ds(0, (SEQ - 1) * 8)], gate_in.at[quarter])

        def rows_of(f):
            return jnp.concatenate(
                [gate_recv[quarter, pl.ds(f, SEQ, 8), :], gate_recv[quarter, pl.ds(4 + f, SEQ, 8), :]],
                axis=1,
            )

        signal = spectrum(rows_of)
        reals, imags = [], []
        for f in range(4):
            rows = slice(f * SEQ, f * SEQ + SEQ)
            real, imag = signal[rows, :TOK], signal[rows, TOK:]
            skip = gain[(quarter * 4 + f) * SEQ + me]
            tap_real = response[rows, :TOK] + skip
            tap_imag = response[rows, TOK:]
            reals.append(real * tap_real - imag * tap_imag)
            imags.append(real * tap_imag + imag * tap_real)
        both = jnp.concatenate(
            [jnp.concatenate(reals, axis=0), jnp.concatenate(imags, axis=0)], axis=1
        )
        high, low = halves(both)
        back = product(high, wide[2]) + product(low, wide[2]) + product(high, wide[3])
        for f in range(4):
            rows = slice(f * SEQ, f * SEQ + SEQ)
            real, imag = back[rows, :TOK], back[rows, TOK:]
            turned = jnp.concatenate(
                [real * twist[2] - imag * twist[3], real * twist[3] + imag * twist[2]], axis=0
            )
            high, low = halves(turned)
            summed = product(tail[...], jnp.concatenate([high, low, high], axis=0))
            asked = far_recv[pl.ds(quarter * 4 + f, SEQ, 16), :]
            swapped = pltpu.roll(asked, 64, 1)
            mine = own_recv[pl.ds(quarter * 4 + f, SEQ, 16), :]
            crossed_mine = pltpu.roll(mine, 64, 1)
            first = jnp.where(is_own, jnp.where(is_low, mine, crossed_mine), 1.0)
            second = jnp.where(is_own, jnp.where(is_low, crossed_mine, mine), 1.0)
            first = jnp.where(is_far, jnp.where(is_low, asked, swapped), first)
            second = jnp.where(is_far, jnp.where(is_low, swapped, asked), second)
            stacked = jnp.concatenate(
                [summed[:, :LANES] * first, summed[:, LANES:] * second], axis=0
            )
            flipped = jnp.transpose(stacked)
            for part in range(4):
                start = part // 2 * 256 + part % 2 * 4 + f
                conv_send[quarter, pl.ds(start, 32, 8), :] = flipped[part * 32 : part * 32 + 32]

        def send(step, inner):
            other = lax.rem(me + 1 + lax.rem(step + 6, SEQ - 1), SEQ)
            pltpu.make_async_remote_copy(
                src_ref=conv_send.at[quarter, pl.ds(pl.multiple_of(other * 8, 8), 8)],
                dst_ref=conv_recv.at[quarter, pl.ds(pl.multiple_of(me * 8, 8), 8)],
                send_sem=conv_out.at[quarter], recv_sem=conv_in.at[quarter],
                device_id=(other, group), device_id_type=MESH,
            ).start()
            return inner

        lax.fori_loop(1, SEQ, send, 0)
        own = pl.ds(pl.multiple_of(me * 8, 8), 8)
        conv_recv[quarter, own, :] = conv_send[quarter, own, :]
        return carry

    lax.fori_loop(0, QUARTERS, convolve, 0)

    wait_bytes(near_recv.at[pl.ds(0, 31)], near_sems.at[1])
    came = (plane - token // 8 - 2 - token % 2 + 16) % 8 >= 4
    wait_bytes(anti_recv.at[pl.ds(0, 32)], anti_sems.at[1])
    crossed = lane % 64 // 8 == (token // 8 + 4) % 8

    lane_plane = lane % 64 // 8
    apart = lane_plane != token // 8

    def far_factor(block, offset):
        packed = anti_recv[:, offset % 2 * 2 + offset // 2, :]
        firsts, seconds = [], []
        for z in range(8):
            rows = packed[z * 8 : z * 8 + 8]
            shift = (z + 4) % 8 * 8 + 128 - 16 * block
            firsts.append(pltpu.roll(rows, lax.rem(shift, LANES), 1))
            seconds.append(pltpu.roll(rows, lax.rem(shift + 56, LANES), 1))
        opened = jnp.where(
            is_low, jnp.concatenate(firsts, axis=0), jnp.concatenate(seconds, axis=0)
        )
        return jnp.where(crossed, opened, 1.0)

    def stage(block, carry):
        lanes = pl.ds(pl.multiple_of(block * LANES, LANES), LANES)
        for offset in range(4):
            asked = jnp.where(apart, near_recv[:, block, offset, :], 1.0)
            out_ref[offset, :, lanes] = jnp.where(came, asked, far_factor(block, offset))
        return carry

    lax.fori_loop(0, 7, stage, 0)
    for offset in range(4):
        gathered = jnp.ones((SEQ, LANES), jnp.float32)
        for block in range(7):
            source = near_recv[:, block, offset, :]
            pieces = []
            for z in range(8):
                shift = ((z + 1 + block) % 8 - z) * 8 % LANES
                pieces.append(pltpu.roll(source[z * 8 : z * 8 + 8], shift, 1))
            here = lane_plane == (token // 8 + 1 + block) % 8
            gathered = jnp.where(here, jnp.concatenate(pieces, axis=0), gathered)
        out_ref[offset, :, pl.ds(7 * LANES, LANES)] = jnp.where(
            came, gathered, far_factor(7, offset)
        )

    def finish(quarter, carry):
        wait_bytes(conv_recv.at[quarter, pl.ds(0, (SEQ - 1) * 8)], conv_in.at[quarter])
        for pair in range(2):
            block = quarter * 2 + pair
            lanes = pl.ds(pl.multiple_of(block * LANES, LANES), LANES)
            for upper in range(2):
                gathered = jnp.concatenate(
                    [conv_recv[quarter, pl.ds(upper * 4 + pair * 2 + own, SEQ, 8), :] for own in range(2)],
                    axis=0,
                )
                turned = jnp.transpose(gathered)
                for lower in range(2):
                    offset = upper * 2 + lower
                    asked = out_ref[offset, :, lanes]
                    out_ref[offset, :, lanes] = asked * turned[lower * 64 : lower * 64 + 64]
        return carry

    lax.fori_loop(0, QUARTERS, finish, 0)

    @pl.when(me < SEQ - 1)
    def _():
        wait_bytes(rim_send, rim_sems.at[0])

    wait_bytes(filt_send.at[pl.ds(0, SEQ - 1)], filt_sems.at[0])
    wait_bytes(filt_all.at[pl.ds(0, GRP - 1)], ring_sems.at[0])
    wait_bytes(near_send.at[pl.ds(0, 31)], near_sems.at[0])
    wait_bytes(own_send.at[pl.ds(0, 7 * 16)], own_sems.at[0])
    wait_bytes(far_send.at[pl.ds(0, (SEQ - 9) * 16)], far_sems.at[0])
    wait_bytes(anti_send, anti_sems.at[0])
    for quarter in range(QUARTERS):
        wait_bytes(gate_send.at[quarter, pl.ds(0, (SEQ - 1) * 8)], gate_out.at[quarter])
        wait_bytes(conv_send.at[quarter, pl.ds(0, (SEQ - 1) * 8)], conv_out.at[quarter])


def body(streams, short_filters, skip_gain, long_filter):
    head_all, tail_all, twists, wide = tables()
    dma = pltpu.SemaphoreType.DMA
    f32 = jnp.float32
    in_hbm = pl.BlockSpec(memory_space=pltpu.HBM)
    return pl.pallas_call(
        kernel,
        out_shape=jax.ShapeDtypeStruct((TOK // SEQ, SEQ, CH), f32),
        in_specs=[in_hbm] * 8,
        out_specs=pl.BlockSpec(memory_space=pltpu.VMEM),
        scratch_shapes=[
            pltpu.VMEM((3, 8, TOK + 8, LANES), f32),
            pltpu.VMEM((3, 3, CH), f32),
            pltpu.SMEM((CH,), f32),
            pltpu.VMEM((64, TOK), f32),
            pltpu.VMEM(head_all.shape, jnp.bfloat16),
            pltpu.VMEM(tail_all.shape, jnp.bfloat16),
            pltpu.VMEM(twists.shape, f32),
            pltpu.VMEM(wide.shape, jnp.bfloat16),
            pltpu.VMEM((3, 8, 8, LANES), f32),
            pltpu.VMEM((3, 8, 2, LANES), f32),
            pltpu.VMEM((3, 8, 2, LANES), f32),
            pltpu.VMEM((SEQ, 2, LANES), f32),
            pltpu.VMEM((SEQ, 2, LANES), f32),
            pltpu.VMEM((GRP, SEQ, TOK), f32),
            pltpu.VMEM((TOK, 2 * TOK), f32),
            pltpu.VMEM((QUARTERS, SEQ * 8, LANES), f32),
            pltpu.VMEM((QUARTERS, SEQ * 8, LANES), f32),
            pltpu.VMEM((SEQ, 7, 4, LANES), f32),
            pltpu.VMEM((SEQ, 7, 4, LANES), f32),
            pltpu.VMEM((SEQ * 16, LANES), f32),
            pltpu.VMEM((SEQ * 16, LANES), f32),
            pltpu.VMEM((32, 4, LANES), f32),
            pltpu.VMEM((SEQ, 4, LANES), f32),
            pltpu.VMEM((SEQ * 16, LANES), f32),
            pltpu.VMEM((SEQ * 16, LANES), f32),
            pltpu.VMEM((QUARTERS, SEQ * 8, LANES), f32),
            pltpu.VMEM((QUARTERS, SEQ * 8, LANES), f32),
            dma((24,)),
            dma((2,)),
            dma((2,)),
            dma((2,)),
            dma((QUARTERS,)),
            dma((QUARTERS,)),
            dma((2,)),
            dma((2,)),
            dma((2,)),
            dma((2,)),
            dma((QUARTERS,)),
            dma((QUARTERS,)),
        ],
        compiler_params=pltpu.CompilerParams(
            collective_id=0, has_side_effects=True, vmem_limit_bytes=48 << 20
        ),
    )(*[pltpu.with_memory_space_constraint(x, pltpu.HBM) for x in (streams, short_filters, skip_gain, long_filter.T, jnp.asarray(head_all), jnp.asarray(tail_all), jnp.asarray(twists), jnp.asarray(wide))])


def solution(mesh):
    return jax.shard_map(
        body,
        mesh=mesh,
        in_specs=(P(None, "seq", "grp"), P(None, None, "grp"), P("grp"), P("seq", "grp")),
        out_specs=P("seq", None, "grp"),
        check_vma=False,
    )
```
